32 devices in a mesh: head: 4 (over y, x), pb: 8 (over z, core).
Axes of the slice: x: 2, y: 2, z: 4, core: 2. Of those that a mesh axis runs over, the one named last changes fastest.
Arguments:
- pair: bfloat16 [512, 512, 128], P('pb', 'head'), may hold values from -6 to 6
- tokens: bfloat16 [512, 768], P('pb'), may hold values from -6 to 6
- token_mask: int32 [512], replicated, may hold values from 0 to 1, as said below
- w_gu: bfloat16 [2, 128, 512], replicated, may hold values from -0.5 to 0.5
- w_down: bfloat16 [2, 256, 128], replicated, may hold values from -0.375 to 0.375
- w_bias: bfloat16 [128, 32], replicated, may hold values from -0.5 to 0.5
- w_q: bfloat16 [2, 768, 768], P(None, None, 'head'), may hold values from -0.21875 to 0.21875
- w_k: bfloat16 [2, 768, 768], P(None, None, 'head'), may hold values from -0.21875 to 0.21875
- w_v: bfloat16 [2, 768, 768], P(None, None, 'head'), may hold values from -0.21875 to 0.21875
- w_gate: bfloat16 [2, 768, 768], P(None, None, 'head'), may hold values from -0.21875 to 0.21875
- w_out: bfloat16 [2, 768, 768], P(None, 'head'), may hold values from -0.875 to 0.875
Outputs:
- updated: bfloat16 [512, 768], P('pb')
The draws below stay inside these ranges and needn't reach their ends.
Inputs may be any that keep to these rules, and one draw needn't show every extreme that they name: `token_mask`: ones on a prefix of the tokens and zeros after it; at least 128 ones and at least one zero.
All inputs are finite; a program needn't handle non-finite values.
Results may differ from the reference program's by a relative error of at most 0.019.
Values may be sent and summed in bfloat16 or wider, within the bound.
A program may use at most 64 MiB of HBM per device.

```python
import jax
import jax.numpy as jnp
from jax import lax

C = 128
FFP = 256
D = 768
H = 16
TRANS = 2
LAYERS = 2
HD = 48
N = 512


def draw_token_mask(key, part):
    real_count = jax.random.randint(jax.random.fold_in(key, 17), (), N // 4, N)
    return (jnp.arange(N) < real_count).astype(jnp.int32)


def draw_tokens(key, part):
    scale_key = jax.random.fold_in(key, 31)
    value_key = jax.random.fold_in(key, 37)
    log_scale = jax.random.uniform(scale_key, (N, 1), jnp.float32, -3.0, 0.4)
    row_scale = jnp.exp(log_scale)
    raw = jax.random.truncated_normal(value_key, -4.0, 4.0, (N, D), jnp.float32)
    return (raw * row_scale).astype(jnp.bfloat16)


def level_of(rng, dims, pieces, smallest, largest):
    loudness = 1.0
    for position, blocks in pieces:
        draws = jax.random.uniform(jax.random.fold_in(jax.random.fold_in(rng, 6), position), (blocks,), jnp.float32, smallest / len(pieces), largest / len(pieces))
        loudness = loudness * jnp.repeat(jnp.exp(draws), dims[position] // blocks).reshape((-1,) + (1,) * (len(dims) - 1 - position))
    return loudness


def noise(rng, shape, scale, most, pieces=(), kind=jnp.bfloat16):
    factor_of = level_of(rng, shape, pieces, -0.22, 0.18) if pieces else 1.0
    result = jax.random.normal(rng, shape, jnp.float32) * scale * factor_of
    return jnp.minimum(jnp.maximum(result, -most), most).astype(kind)


def setup_inputs(seed: int = 0) -> dict:
    streams_of = jax.random.split(jax.random.key(seed), 12)
    return {
        "pair": noise(streams_of[0], (N, N, C), 1.0, 6.0, ((0, 8), (1, 4))),
        "tokens": draw_tokens(jax.random.fold_in(streams_of[11], 71), 0),
        "token_mask": draw_token_mask(jax.random.fold_in(streams_of[11], 71), 0),
        "w_gu": noise(streams_of[3], (TRANS, C, 2 * FFP), C ** -0.5, 0.5),
        "w_down": noise(streams_of[4], (TRANS, FFP, C), FFP ** -0.5, 0.375),
        "w_bias": noise(streams_of[5], (C, LAYERS * H), C ** -0.5, 0.5),
        "w_q": noise(streams_of[6], (LAYERS, D, D), D ** -0.5, 0.21875, ((2, 4),)),
        "w_k": noise(streams_of[7], (LAYERS, D, D), D ** -0.5, 0.21875, ((2, 4),)),
        "w_v": noise(streams_of[8], (LAYERS, D, D), D ** -0.5, 0.21875, ((2, 4),)),
        "w_gate": noise(streams_of[9], (LAYERS, D, D), D ** -0.5, 0.21875, ((2, 4),)),
        "w_out": noise(streams_of[10], (LAYERS, D, D), (D // 16) ** -0.5, 0.875, ((1, 4),)),
    }


def normalize(values):
    values = values.astype(jnp.float32)
    center = values - lax.optimization_barrier(jnp.mean(values, axis=-1, keepdims=True))
    spread = lax.optimization_barrier(jnp.mean(center * center, axis=-1, keepdims=True))
    return center * lax.rsqrt(spread + 1e-05)

def transition(pair_rows, w_updown, w_back):
    normed = normalize(pair_rows).astype(jnp.bfloat16)
    mixed = jnp.dot(normed, w_updown, preferred_element_type=jnp.float32)
    hidden = (jax.nn.silu(mixed[:, :FFP]) * mixed[:, FFP:]).astype(jnp.bfloat16)
    summed = pair_rows.astype(jnp.float32) + jnp.dot(hidden, w_back, preferred_element_type=jnp.float32)
    return summed.astype(jnp.bfloat16)

def reference(pair, tokens, token_mask, w_gu, w_down, w_bias, w_q, w_k, w_v, w_gate, w_out):

    def one_row(pair_row):
        current = pair_row
        for section_index in range(TRANS):
            current = transition(current, w_gu[section_index], w_down[section_index])
        normed = normalize(current).astype(jnp.bfloat16)
        return jnp.dot(normed, w_bias, preferred_element_type=jnp.float32).astype(jnp.bfloat16)
    bias_all = lax.map(one_row, pair).reshape(N, N, LAYERS, H)
    is_real = token_mask == 1
    real_rows = is_real.astype(jnp.float32)
    state = tokens.astype(jnp.float32)
    for layer_index in range(LAYERS):
        normed = normalize(state).astype(jnp.bfloat16)
        queries = jnp.dot(normed, w_q[layer_index], preferred_element_type=jnp.float32).astype(jnp.bfloat16)
        key_proj = jnp.dot(normed, w_k[layer_index], preferred_element_type=jnp.float32).astype(jnp.bfloat16)
        value_proj = jnp.dot(normed, w_v[layer_index], preferred_element_type=jnp.float32).astype(jnp.bfloat16)
        gate_vals = jnp.dot(normed, w_gate[layer_index], preferred_element_type=jnp.float32).astype(jnp.bfloat16)
        query_heads = queries.astype(jnp.float32).reshape(N, H, HD)
        key_heads = key_proj.astype(jnp.float32).reshape(N, H, HD)
        value_heads = value_proj.astype(jnp.float32).reshape(N, H, HD)
        scores = jnp.einsum('ihd,jhd->hij', query_heads, key_heads) * (1.0 / HD ** 0.5)
        scores = scores + jnp.transpose(bias_all[:, :, layer_index, :], (2, 0, 1)).astype(jnp.float32)
        scores = jnp.where(is_real[None, None, :], scores, -1e+30)
        weights = jax.nn.softmax(scores, axis=-1)
        attended = jnp.einsum('hij,jhd->ihd', weights, value_heads).reshape(N, D)
        gated = (attended * jax.nn.sigmoid(gate_vals.astype(jnp.float32))).astype(jnp.bfloat16)
        update = jnp.dot(gated, w_out[layer_index], preferred_element_type=jnp.float32)
        state = state + real_rows[:, None] * update
    return state.astype(jnp.bfloat16)
```

```python
import functools

import jax
import jax.numpy as jnp
from jax import lax
from jax.experimental import pallas as pl
from jax.experimental.pallas import tpu as pltpu
from jax.sharding import PartitionSpec as P

TRANS = 2
LAYERS = 2
HD = 48
CORES = 2
ROW_TILE = 16
GROUP = 8
LANES = 128
F32 = jnp.float32
BF16 = jnp.bfloat16


def normalize(values):
    inverse = 1.0 / values.shape[-1]
    center = values - jnp.sum(values, axis=-1, keepdims=True) * inverse
    spread = jnp.sum(center * center, axis=-1, keepdims=True) * inverse
    return center * lax.rsqrt(spread + 1e-05)


def scale_rows(center):
    inverse = 1.0 / center.shape[-1]
    spread = jnp.sum(center * center, axis=-1, keepdims=True) * inverse
    return (center * lax.rsqrt(spread + 1e-05)).astype(BF16)


def matmul(left, right):
    return jnp.dot(left, right, preferred_element_type=F32)


def matmul_t(left, right):
    return lax.dot_general(left, right, (((1,), (1,)), ((), ())), preferred_element_type=F32)


def pair_chunks(rows):
    tiles = rows // ROW_TILE
    counts = [1, tiles - 2, 1] if tiles > 2 else [1] * tiles
    starts = [sum(counts[:n]) for n in range(len(counts))]
    return [(a * ROW_TILE, c * ROW_TILE) for a, c in zip(starts, counts)]


def token_parts(rows):
    last = pair_chunks(rows)[-1][0]
    return [(0, last), (last, rows - last)]


def step_kernel(
    head_count,
    pb_count,
    pair_hbm,
    tokens_ref,
    mask_ref,
    gu_ref,
    down_ref,
    bias_w_ref,
    q_hbm,
    k_hbm,
    v_hbm,
    gate_hbm,
    out_hbm,
    result_ref,
    pair_v,
    gu_v,
    down_v,
    wide_w,
    out_w,
    bias_out,
    bias_in,
    kv_all,
    query_gate,
    gated_all,
    state_v,
    pair_sem,
    weight_sem,
    bias_send,
    bias_recv,
    kv_send,
    kv_recv,
    fwd_send,
    fwd_recv,
    gated_send,
    gated_recv,
    out_send,
    out_recv,
    out_fwd_send,
    out_fwd_recv,
):
    rows, cols, channels = pair_hbm.shape
    width = q_hbm.shape[1]
    features = tokens_ref.shape[1]
    local_heads = width // HD
    heads_all = local_heads * head_count
    half_width = width // CORES
    chips = pb_count // CORES
    col_blocks = cols // LANES
    hidden = down_ref.shape[1]
    chunks = pair_chunks(rows)
    parts = token_parts(rows)
    kv_parts = [[(0, rows)]] + [parts] * (LAYERS - 1)
    gated_parts = [parts] * (LAYERS - 1) + [[(0, rows)]]

    head = lax.axis_index("head")
    pb = lax.axis_index("pb")
    core = lax.rem(pb, CORES)
    chip = pb // CORES
    partner = chip * CORES + (1 - core)

    def head_peer(k):
        return lax.rem(head + k, head_count)

    def chip_peer(d):
        return lax.rem(chip + d, chips) * CORES + core

    def chip_source(d):
        return lax.rem(chip + chips - d, chips) * CORES + core

    def projection_copies(layer):
        return [
            pltpu.make_async_copy(
                source.at[layer],
                wide_w.at[layer, index * width : (index + 1) * width],
                weight_sem.at[layer, index],
            )
            for index, source in enumerate((k_hbm, v_hbm, q_hbm, gate_hbm))
        ]

    def own_out_copies(layer):
        return [
            pltpu.make_async_copy(
                out_hbm.at[layer, part * half_width : (part + 1) * half_width],
                out_w.at[layer, head, part],
                weight_sem.at[layer, 4 + part],
            )
            for part in range(CORES)
        ]

    def pair_copy(n):
        first, count = chunks[n]
        return pltpu.make_async_copy(
            pair_hbm.at[first : first + count], pair_v.at[first : first + count], pair_sem.at[n]
        )

    pair_copy(0).start()
    for copy in projection_copies(0):
        copy.start()
    for n in range(1, len(chunks)):
        pair_copy(n).start()
    for layer in range(LAYERS):
        for copy in own_out_copies(layer) + (projection_copies(layer) if layer else []):
            copy.start()

    barrier = pltpu.get_barrier_semaphore()
    for k in range(1, head_count):
        pl.semaphore_signal(
            barrier, inc=1, device_id=(head_peer(k), pb), device_id_type=pl.DeviceIdType.MESH
        )
    for d in range(1, chips):
        pl.semaphore_signal(
            barrier, inc=1, device_id=(head, chip_peer(d)), device_id_type=pl.DeviceIdType.MESH
        )
    pl.semaphore_signal(
        barrier, inc=1, device_id=(head, partner), device_id_type=pl.DeviceIdType.MESH
    )

    def remote(source, target, send, recv, where):
        return pltpu.make_async_remote_copy(
            src_ref=source,
            dst_ref=target,
            send_sem=send,
            recv_sem=recv,
            device_id=where,
            device_id_type=pl.DeviceIdType.MESH,
        )

    def span(part):
        return slice(part[0], part[0] + part[1])

    def kv_copy(layer, p, d):
        block = kv_all.at[layer, pb, span(kv_parts[layer][p])]
        return remote(
            block, block, kv_send.at[layer, p, d], kv_recv.at[layer, p, d], (head, chip_peer(d))
        )

    def kv_forward(layer, p, d):
        block = kv_all.at[layer, chip_source(d), span(kv_parts[layer][p])]
        return remote(
            block, block, fwd_send.at[layer, p, d], fwd_recv.at[layer, p, d], (head, partner)
        )

    def out_copy(layer, k):
        return remote(
            out_hbm.at[layer, pl.ds(pl.multiple_of(core * half_width, half_width), half_width)],
            out_w.at[layer, head, core],
            out_send.at[layer, k],
            out_recv.at[layer, k],
            (head_peer(k), pb),
        )

    def out_forward(layer, k):
        block = out_w.at[layer, lax.rem(head + head_count - k, head_count), core]
        return remote(
            block, block, out_fwd_send.at[layer, k], out_fwd_recv.at[layer, k], (head, partner)
        )

    def forward_out(layer):
        for k in range(1, head_count):
            out_copy(layer, k).wait_recv()
            out_forward(layer, k).start()

    def gated_copy(layer, p, k):
        block = gated_all.at[layer, head, span(gated_parts[layer][p])]
        return remote(
            block, block, gated_send.at[layer, p, k], gated_recv.at[layer, p, k], (head_peer(k), pb)
        )

    def bias_copy(n, layer, k):
        where = span(chunks[n])
        return remote(
            bias_out.at[head_peer(k), layer, :, where],
            bias_in.at[head, layer, :, where],
            bias_send.at[n, layer, k],
            bias_recv.at[n, layer, k],
            (head_peer(k), pb),
        )

    def project(layer, p, normed):
        where = span(kv_parts[layer][p])
        kv_all[layer, pb, where] = matmul_t(normed, wide_w[layer, : 2 * width]).astype(BF16)

    def send_kv(layer, p):
        for d in range(1, chips):
            kv_copy(layer, p, d).start()
        kv_forward(layer, p, 0).start()

    def project_own(layer, p, normed):
        where = span(kv_parts[layer][p])
        query_gate[where] = matmul_t(normed, wide_w[layer, 2 * width :]).astype(BF16)

    def forward_kv(layer, p):
        for d in range(1, chips):
            kv_copy(layer, p, d).wait_recv()
            kv_forward(layer, p, d).start()

    def finish_kv(layer, p):
        for d in range(chips):
            kv_forward(layer, p, d).wait_recv()

    for section in range(TRANS):
        gu_v[section, :, :hidden] = (gu_ref[section, :, :hidden].astype(F32) * 0.5).astype(BF16)
        gu_v[section, :, hidden:] = gu_ref[section, :, hidden:]
        down = down_ref[section].astype(F32)
        level = jnp.sum(down, axis=-1, keepdims=True) * (1.0 / channels)
        down_v[section] = (down - level).astype(BF16)
    bias_w = bias_w_ref[...]

    def pair_block(first_row, row_count, first_col):
        blocks = []
        for start in range(0, row_count, GROUP):
            count = min(GROUP, row_count - start)
            wide = (
                pair_v[pl.ds(first_row + start, count), pl.ds(first_col, LANES), :]
                .reshape(count * LANES, channels)
                .astype(F32)
            )
            blocks.append(wide - jnp.sum(wide, axis=-1, keepdims=True) * (1.0 / channels))
        for section in range(TRANS):
            for n, center in enumerate(blocks):
                mixed = matmul(scale_rows(center), gu_v[section])
                gate = mixed[:, :hidden]
                units = ((gate + gate * jnp.tanh(gate)) * mixed[:, hidden:]).astype(BF16)
                blocks[n] = center + matmul(units, down_v[section])
        planes = []
        for center in blocks:
            projected = matmul_t(bias_w, scale_rows(center))
            planes += [
                projected[:, i : i + LANES] for i in range(0, projected.shape[1], LANES)
            ]
        by_head = jnp.transpose(jnp.stack(planes, axis=0), (1, 0, 2)).astype(BF16)
        for layer in range(LAYERS):
            for target in range(head_count):
                start = layer * heads_all + target * local_heads
                bias_out[
                    target, layer, :, pl.ds(first_row, row_count), pl.ds(first_col, LANES)
                ] = by_head[start : start + local_heads]
        bias_in[head, :, :, pl.ds(first_row, row_count), pl.ds(first_col, LANES)] = bias_out[
            head, :, :, pl.ds(first_row, row_count), pl.ds(first_col, LANES)
        ]

    def pair_step(n):
        pair_copy(n).wait()
        first_row, row_count = chunks[n]
        if col_blocks == 1:
            pair_block(first_row, row_count, 0)
        else:

            def one(block, carry):
                pair_block(first_row, row_count, pl.multiple_of(block * LANES, LANES))
                return carry

            lax.fori_loop(0, col_blocks, one, 0)

    def send_bias(n):
        for layer in range(LAYERS):
            for k in range(1, head_count):
                bias_copy(n, layer, k).start()

    def wait_bias(layer, part):
        for n, (first, count) in enumerate(chunks):
            if part[0] <= first < part[0] + part[1]:
                for k in range(1, head_count):
                    bias_copy(n, layer, k).wait_recv()

    pair_step(0)
    for copy in projection_copies(0):
        copy.wait()
    normed = normalize(tokens_ref[...].astype(F32)).astype(BF16)
    project(0, 0, normed)
    pl.semaphore_wait(barrier, head_count + chips - 1)
    send_bias(0)
    send_kv(0, 0)
    for k in range(1, head_count):
        out_copy(0, k).start()
    project_own(0, 0, normed)
    for n in range(1, len(chunks)):
        pair_step(n)
        send_bias(n)
        if n == len(chunks) - 2:
            forward_kv(0, 0)
            forward_out(0)
    if len(chunks) < 3:
        forward_kv(0, 0)
        forward_out(0)

    mask_row = mask_ref[...]
    real_count = jnp.sum(mask_row.astype(F32), axis=1, keepdims=True)
    is_real = mask_row == 1
    row_index = (lax.broadcasted_iota(jnp.int32, (rows, 1), 0) + pb * rows).astype(F32)
    row_real = (row_index < real_count).astype(F32)
    scale = 1.0 / HD**0.5

    def attend(layer, part):
        first, count = part
        keys_values = kv_all[layer].reshape(pb_count * rows, 2 * width)
        queries = query_gate[span(part)]
        lane = lax.broadcasted_iota(jnp.int32, (count, 2 * width), 1)
        spread_q = jnp.concatenate(
            [
                jnp.where((lane >= h * HD) & (lane < (h + 1) * HD), queries, jnp.zeros_like(queries))
                for h in range(local_heads)
            ],
            axis=0,
        )
        scores = matmul_t(spread_q, keys_values) * scale
        wait_bias(layer, part)
        bias = jnp.concatenate(
            [
                bias_in[source, layer, :, span(part)].reshape(local_heads * count, cols)
                for source in range(head_count)
            ],
            axis=1,
        )
        scores = scores + bias.astype(F32)
        scores = jnp.where(is_real, scores, -1e30)
        peak = jnp.max(scores, axis=1, keepdims=True)
        weights = jnp.exp(scores - peak)
        total = jnp.sum(weights, axis=1, keepdims=True)
        mixed = matmul(weights.astype(BF16), keys_values) / total
        attended = jnp.zeros((count, 2 * width), F32)
        for h in range(local_heads):
            keep = (lane >= width + h * HD) & (lane < width + (h + 1) * HD)
            attended = attended + jnp.where(keep, mixed[h * count : (h + 1) * count], 0.0)
        gated = (attended * jax.nn.sigmoid(queries.astype(F32))).astype(BF16)
        gated_all[layer, head, span(part)] = gated[:, width:]

    state_v[...] = tokens_ref[...].astype(F32)
    for layer in range(LAYERS):
        for p in range(len(kv_parts[layer])):
            if layer:
                forward_kv(layer, p)
            finish_kv(layer, p)
        for p, part in enumerate(gated_parts[layer]):
            attend(layer, part)
            for k in range(1, head_count):
                gated_copy(layer, p, k).start()
        if layer:
            forward_out(layer)
        for k in range(1, head_count):
            out_forward(layer, k).wait_recv()
        for copy in own_out_copies(layer):
            copy.wait()
        for p, part in enumerate(gated_parts[layer]):
            where = span(part)
            for k in range(1, head_count):
                gated_copy(layer, p, k).wait_recv()
            gathered = jnp.concatenate(
                [gated_all[layer, h, where] for h in range(head_count)], axis=1
            )
            update = matmul(gathered, out_w[layer].reshape(head_count * width, features))
            state = state_v[where] + row_real[where] * update
            if layer == LAYERS - 1:
                result_ref[where] = state.astype(BF16)
            else:
                if not p:
                    for copy in projection_copies(layer + 1):
                        copy.wait()
                state_v[where] = state
                normed = normalize(state).astype(BF16)
                project(layer + 1, p, normed)
                send_kv(layer + 1, p)
                project_own(layer + 1, p, normed)
        if layer + 1 < LAYERS:
            for k in range(1, head_count):
                out_copy(layer + 1, k).start()

    for layer in range(LAYERS):
        for k in range(1, head_count):
            for n in range(len(chunks)):
                bias_copy(n, layer, k).wait_send()
            for p in range(len(gated_parts[layer])):
                gated_copy(layer, p, k).wait_send()
            out_copy(layer, k).wait_send()
            out_forward(layer, k).wait_send()
        for p in range(len(kv_parts[layer])):
            for d in range(chips):
                kv_forward(layer, p, d).wait_send()
                if d:
                    kv_copy(layer, p, d).wait_send()


def on_device(
    head_count, pb_count, pair, tokens, token_mask, w_gu, w_down, w_bias, w_q, w_k, w_v, w_gate, w_out
):
    rows, cols, channels = pair.shape
    width = w_q.shape[2]
    features = tokens.shape[1]
    local_heads = width // HD
    chips = pb_count // CORES
    chunks = len(pair_chunks(rows))
    parts = len(token_parts(rows))
    vmem = pl.BlockSpec(memory_space=pltpu.VMEM)
    anywhere = pl.BlockSpec(memory_space=pl.ANY)
    dma = pltpu.SemaphoreType.DMA
    bias_shape = (head_count, LAYERS, local_heads, rows, cols)
    return pl.pallas_call(
        functools.partial(step_kernel, head_count, pb_count),
        out_shape=jax.ShapeDtypeStruct((rows, features), BF16),
        in_specs=[anywhere] + [vmem] * 5 + [anywhere] * 5,
        out_specs=vmem,
        scratch_shapes=[
            pltpu.VMEM(pair.shape, BF16),
            pltpu.VMEM(w_gu.shape, BF16),
            pltpu.VMEM(w_down.shape, BF16),
            pltpu.VMEM((LAYERS, 4 * width, features), BF16),
            pltpu.VMEM((LAYERS, head_count, CORES, width // CORES, features), BF16),
            pltpu.VMEM(bias_shape, BF16),
            pltpu.VMEM(bias_shape, BF16),
            pltpu.VMEM((LAYERS, pb_count, rows, 2 * width), BF16),
            pltpu.VMEM((rows, 2 * width), BF16),
            pltpu.VMEM((LAYERS, head_count, rows, width), BF16),
            pltpu.VMEM((rows, features), F32),
            dma((chunks,)),
            dma((LAYERS, 4 + CORES)),
            dma((chunks, LAYERS, head_count)),
            dma((chunks, LAYERS, head_count)),
            dma((LAYERS, parts, chips)),
            dma((LAYERS, parts, chips)),
            dma((LAYERS, parts, chips)),
            dma((LAYERS, parts, chips)),
            dma((LAYERS, parts, head_count)),
            dma((LAYERS, parts, head_count)),
            dma((LAYERS, head_count)),
            dma((LAYERS, head_count)),
            dma((LAYERS, head_count)),
            dma((LAYERS, head_count)),
        ],
        compiler_params=pltpu.CompilerParams(
            collective_id=0, has_side_effects=True, vmem_limit_bytes=60 * 1024 * 1024
        ),
        name="diffusion_step",
    )(
        pair,
        tokens,
        token_mask.reshape(1, -1),
        w_gu,
        w_down,
        w_bias.T,
        jnp.swapaxes(w_q, 1, 2),
        jnp.swapaxes(w_k, 1, 2),
        jnp.swapaxes(w_v, 1, 2),
        jnp.swapaxes(w_gate, 1, 2),
        w_out,
    )


def solution(mesh):
    placed = (
        P("pb", "head", None),
        P("pb", None),
        P(),
        P(),
        P(),
        P(),
        P(None, None, "head"),
        P(None, None, "head"),
        P(None, None, "head"),
        P(None, None, "head"),
        P(None, "head", None),
    )
    return jax.shard_map(
        functools.partial(on_device, mesh.shape["head"], mesh.shape["pb"]),
        mesh=mesh,
        in_specs=placed,
        out_specs=P("pb", None),
        check_vma=False,
    )
```

```python
import functools

import jax
import jax.numpy as jnp
from jax import lax
from jax.experimental import pallas as pl
from jax.experimental.pallas import tpu as pltpu
from jax.sharding import PartitionSpec as P

TRANS = 2
LAYERS = 2
HD = 48
CORES = 2
ROW_TILE = 16
GROUP = 8
LANES = 128
F32 = jnp.float32
BF16 = jnp.bfloat16


def normalize(values):
    inverse = 1.0 / values.shape[-1]
    center = values - jnp.sum(values, axis=-1, keepdims=True) * inverse
    spread = jnp.sum(center * center, axis=-1, keepdims=True) * inverse
    return center * lax.rsqrt(spread + 1e-05)


def scale_rows(center):
    inverse = 1.0 / center.shape[-1]
    spread = jnp.sum(center * center, axis=-1, keepdims=True) * inverse
    return (center * lax.rsqrt(spread + 1e-05)).astype(BF16)


def matmul(left, right):
    return jnp.dot(left, right, preferred_element_type=F32)


def matmul_t(left, right):
    return lax.dot_general(left, right, (((1,), (1,)), ((), ())), preferred_element_type=F32)


def pair_chunks(rows):
    tiles = rows // ROW_TILE
    counts = [1, tiles - 2, 1] if tiles > 2 else [1] * tiles
    starts = [sum(counts[:n]) for n in range(len(counts))]
    return [(a * ROW_TILE, c * ROW_TILE) for a, c in zip(starts, counts)]


def token_parts(rows):
    last = pair_chunks(rows)[-1][0]
    return [(0, last), (last, rows - last)]


def step_kernel(
    head_count,
    pb_count,
    pair_hbm,
    tokens_ref,
    mask_ref,
    gu_ref,
    down_ref,
    bias_w_ref,
    q_hbm,
    k_hbm,
    v_hbm,
    gate_hbm,
    out_hbm,
    result_ref,
    pair_v,
    gu_v,
    down_v,
    wide_w,
    out_w,
    bias_out,
    bias_in,
    kv_all,
    query_gate,
    gated_all,
    state_v,
    pair_sem,
    weight_sem,
    bias_send,
    bias_recv,
    kv_send,
    kv_recv,
    fwd_send,
    fwd_recv,
    gated_send,
    gated_recv,
    out_send,
    out_recv,
    out_fwd_send,
    out_fwd_recv,
):
    rows, cols, channels = pair_hbm.shape
    width = q_hbm.shape[1]
    features = tokens_ref.shape[1]
    local_heads = width // HD
    heads_all = local_heads * head_count
    half_width = width // CORES
    chips = pb_count // CORES
    col_blocks = cols // LANES
    hidden = down_ref.shape[1]
    chunks = pair_chunks(rows)
    parts = token_parts(rows)
    kv_parts = [[(0, rows)]] + [parts] * (LAYERS - 1)
    gated_parts = [parts] * (LAYERS - 1) + [[(0, rows)]]

    head = lax.axis_index("head")
    pb = lax.axis_index("pb")
    core = lax.rem(pb, CORES)
    chip = pb // CORES
    partner = chip * CORES + (1 - core)

    def head_peer(k):
        return lax.rem(head + k, head_count)

    def chip_peer(d):
        return lax.rem(chip + d, chips) * CORES + core

    def chip_source(d):
        return lax.rem(chip + chips - d, chips) * CORES + core

    def projection_copies(layer):
        return [
            pltpu.make_async_copy(
                source.at[layer],
                wide_w.at[layer, index * width : (index + 1) * width],
                weight_sem.at[layer, index],
            )
            for index, source in enumerate((k_hbm, v_hbm, q_hbm, gate_hbm))
        ]

    def own_out_copies(layer):
        return [
            pltpu.make_async_copy(
                out_hbm.at[layer, part * half_width : (part + 1) * half_width],
                out_w.at[layer, head, part],
                weight_sem.at[layer, 4 + part],
            )
            for part in range(CORES)
        ]

    def pair_copy(n):
        first, count = chunks[n]
        return pltpu.make_async_copy(
            pair_hbm.at[first : first + count], pair_v.at[first : first + count], pair_sem.at[n]
        )

    pair_copy(0).start()
    for copy in projection_copies(0):
        copy.start()
    for n in range(1, len(chunks)):
        pair_copy(n).start()
    for layer in range(LAYERS):
        for copy in own_out_copies(layer) + (projection_copies(layer) if layer else []):
            copy.start()

    barrier = pltpu.get_barrier_semaphore()
    for k in range(1, head_count):
        pl.semaphore_signal(
            barrier, inc=1, device_id=(head_peer(k), pb), device_id_type=pl.DeviceIdType.MESH
        )
    for d in range(1, chips):
        pl.semaphore_signal(
            barrier, inc=1, device_id=(head, chip_peer(d)), device_id_type=pl.DeviceIdType.MESH
        )
    pl.semaphore_signal(
        barrier, inc=1, device_id=(head, partner), device_id_type=pl.DeviceIdType.MESH
    )

    def remote(source, target, send, recv, where):
        return pltpu.make_async_remote_copy(
            src_ref=source,
            dst_ref=target,
            send_sem=send,
            recv_sem=recv,
            device_id=where,
            device_id_type=pl.DeviceIdType.MESH,
        )

    def span(part):
        return slice(part[0], part[0] + part[1])

    def kv_copy(layer, p, d):
        block = kv_all.at[layer, pb, span(kv_parts[layer][p])]
        return remote(
            block, block, kv_send.at[layer, p, d], kv_recv.at[layer, p, d], (head, chip_peer(d))
        )

    def kv_forward(layer, p, d):
        block = kv_all.at[layer, chip_source(d), span(kv_parts[layer][p])]
        return remote(
            block, block, fwd_send.at[layer, p, d], fwd_recv.at[layer, p, d], (head, partner)
        )

    def out_copy(layer, k):
        return remote(
            out_hbm.at[layer, pl.ds(pl.multiple_of(core * half_width, half_width), half_width)],
            out_w.at[layer, head, core],
            out_send.at[layer, k],
            out_recv.at[layer, k],
            (head_peer(k), pb),
        )

    def out_forward(layer, k):
        block = out_w.at[layer, lax.rem(head + head_count - k, head_count), core]
        return remote(
            block, block, out_fwd_send.at[layer, k], out_fwd_recv.at[layer, k], (head, partner)
        )

    def forward_out(layer):
        for k in range(1, head_count):
            out_copy(layer, k).wait_recv()
            out_forward(layer, k).start()

    def gated_copy(layer, p, k):
        block = gated_all.at[layer, head, span(gated_parts[layer][p])]
        return remote(
            block, block, gated_send.at[layer, p, k], gated_recv.at[layer, p, k], (head_peer(k), pb)
        )

    def bias_copy(n, layer, k):
        first, count = chunks[n]
        where = slice(first // ROW_TILE, (first + count) // ROW_TILE)
        return remote(
            bias_out.at[head_peer(k), layer, where],
            bias_in.at[head, layer, where],
            bias_send.at[n, layer, k],
            bias_recv.at[n, layer, k],
            (head_peer(k), pb),
        )

    def project(layer, p, normed):
        where = span(kv_parts[layer][p])
        kv_all[layer, pb, where] = matmul_t(normed, wide_w[layer, : 2 * width]).astype(BF16)

    def send_kv(layer, p):
        for d in range(1, chips):
            kv_copy(layer, p, d).start()
        kv_forward(layer, p, 0).start()

    def project_own(layer, p, normed):
        where = span(kv_parts[layer][p])
        query_gate[where] = matmul_t(normed, wide_w[layer, 2 * width :]).astype(BF16)

    def forward_kv(layer, p):
        for d in range(1, chips):
            kv_copy(layer, p, d).wait_recv()
            kv_forward(layer, p, d).start()

    def finish_kv(layer, p):
        for d in range(chips):
            kv_forward(layer, p, d).wait_recv()

    for section in range(TRANS):
        gu_v[section, :, :hidden] = (gu_ref[section, :, :hidden].astype(F32) * 0.5).astype(BF16)
        gu_v[section, :, hidden:] = gu_ref[section, :, hidden:]
        down = down_ref[section].astype(F32)
        level = jnp.sum(down, axis=-1, keepdims=True) * (1.0 / channels)
        down_v[section] = (down - level).astype(BF16)
    bias_w = bias_w_ref[...]

    def pair_block(first_row, row_count, first_col):
        blocks = []
        for start in range(0, row_count, GROUP):
            count = min(GROUP, row_count - start)
            wide = (
                pair_v[pl.ds(first_row + start, count), pl.ds(first_col, LANES), :]
                .reshape(count * LANES, channels)
                .astype(F32)
            )
            blocks.append(wide - jnp.sum(wide, axis=-1, keepdims=True) * (1.0 / channels))
        for section in range(TRANS):
            for n, center in enumerate(blocks):
                mixed = matmul(scale_rows(center), gu_v[section])
                gate = mixed[:, :hidden]
                units = ((gate + gate * jnp.tanh(gate)) * mixed[:, hidden:]).astype(BF16)
                blocks[n] = center + matmul(units, down_v[section])
        planes = []
        for center in blocks:
            projected = matmul_t(bias_w, scale_rows(center))
            planes += [
                projected[:, i : i + LANES] for i in range(0, projected.shape[1], LANES)
            ]
        by_head = jnp.transpose(jnp.stack(planes, axis=0), (1, 0, 2)).astype(BF16)
        for layer in range(LAYERS):
            for target in range(head_count):
                start = layer * heads_all + target * local_heads
                for row in range(0, row_count, ROW_TILE):
                    tile = (first_row + row) // ROW_TILE
                    bias_out[target, layer, tile, :, :, pl.ds(first_col, LANES)] = by_head[
                        start : start + local_heads, row : row + ROW_TILE
                    ]
        tiles = slice(first_row // ROW_TILE, (first_row + row_count) // ROW_TILE)
        bias_in[head, :, tiles, :, :, pl.ds(first_col, LANES)] = bias_out[
            head, :, tiles, :, :, pl.ds(first_col, LANES)
        ]

    def pair_step(n):
        pair_copy(n).wait()
        first_row, row_count = chunks[n]
        if col_blocks == 1:
            pair_block(first_row, row_count, 0)
        else:

            def one(block, carry):
                pair_block(first_row, row_count, pl.multiple_of(block * LANES, LANES))
                return carry

            lax.fori_loop(0, col_blocks, one, 0)

    def send_bias(n, layer):
        for k in range(1, head_count):
            bias_copy(n, layer, k).start()

    def wait_bias(layer, part):
        for n, (first, count) in enumerate(chunks):
            if part[0] <= first < part[0] + part[1]:
                for k in range(1, head_count):
                    bias_copy(n, layer, k).wait_recv()

    pair_step(0)
    for copy in projection_copies(0):
        copy.wait()
    normed = normalize(tokens_ref[...].astype(F32)).astype(BF16)
    project(0, 0, normed)
    pl.semaphore_wait(barrier, head_count + chips - 1)
    send_bias(0, 0)
    send_kv(0, 0)
    for k in range(1, head_count):
        out_copy(0, k).start()
    for n in range(1, len(chunks)):
        pair_step(n)
        send_bias(n, 0)
    forward_kv(0, 0)
    for layer in range(1, LAYERS):
        for n in range(len(chunks)):
            send_bias(n, layer)
    project_own(0, 0, normed)
    forward_out(0)

    mask_row = mask_ref[...]
    real_count = jnp.sum(mask_row.astype(F32), axis=1, keepdims=True)
    is_real = mask_row == 1
    row_index = (lax.broadcasted_iota(jnp.int32, (rows, 1), 0) + pb * rows).astype(F32)
    row_real = (row_index < real_count).astype(F32)
    scale = 1.0 / HD**0.5

    def attend(layer, part):
        first, count = part
        keys_values = kv_all[layer].reshape(pb_count * rows, 2 * width)
        queries = query_gate[span(part)]
        lane = lax.broadcasted_iota(jnp.int32, (ROW_TILE, 2 * width), 1)
        tiles = range(0, count, ROW_TILE)
        spread_q = jnp.concatenate(
            [
                jnp.where(
                    (lane >= h * HD) & (lane < (h + 1) * HD), queries[t : t + ROW_TILE], jnp.zeros((), BF16)
                )
                for t in tiles
                for h in range(local_heads)
            ],
            axis=0,
        )
        scores = matmul_t(spread_q, keys_values) * scale
        wait_bias(layer, part)
        bias = jnp.concatenate(
            [
                bias_in[
                    source, layer, first // ROW_TILE : (first + count) // ROW_TILE
                ].reshape(local_heads * count, cols)
                for source in range(head_count)
            ],
            axis=1,
        )
        scores = scores + bias.astype(F32)
        scores = jnp.where(is_real, scores, -1e30)
        peak = jnp.max(scores, axis=1, keepdims=True)
        weights = jnp.exp(scores - peak)
        total = jnp.sum(weights, axis=1, keepdims=True)
        mixed = matmul(weights.astype(BF16), keys_values) / total
        rows_of = []
        for t in tiles:
            attended = jnp.zeros((ROW_TILE, 2 * width), F32)
            for h in range(local_heads):
                keep = (lane >= width + h * HD) & (lane < width + (h + 1) * HD)
                start = t * local_heads + h * ROW_TILE
                attended = attended + jnp.where(keep, mixed[start : start + ROW_TILE], 0.0)
            rows_of.append(attended)
        attended = jnp.concatenate(rows_of, axis=0)
        gated = (attended * jax.nn.sigmoid(queries.astype(F32))).astype(BF16)
        gated_all[layer, head, span(part)] = gated[:, width:]

    state_v[...] = tokens_ref[...].astype(F32)
    for layer in range(LAYERS):
        for p in range(len(kv_parts[layer])):
            if layer:
                forward_kv(layer, p)
            finish_kv(layer, p)
        for p, part in enumerate(gated_parts[layer]):
            attend(layer, part)
            for k in range(1, head_count):
                gated_copy(layer, p, k).start()
        if layer + 1 < LAYERS:
            for k in range(1, head_count):
                out_copy(layer + 1, k).start()
        if layer:
            forward_out(layer)
        for k in range(1, head_count):
            out_forward(layer, k).wait_recv()
        for copy in own_out_copies(layer):
            copy.wait()
        for p, part in enumerate(gated_parts[layer]):
            where = span(part)
            for k in range(1, head_count):
                gated_copy(layer, p, k).wait_recv()
            gathered = jnp.concatenate(
                [gated_all[layer, h, where] for h in range(head_count)], axis=1
            )
            update = matmul(gathered, out_w[layer].reshape(head_count * width, features))
            state = state_v[where] + row_real[where] * update
            if layer == LAYERS - 1:
                result_ref[where] = state.astype(BF16)
            else:
                if not p:
                    for copy in projection_copies(layer + 1):
                        copy.wait()
                state_v[where] = state
                normed = normalize(state).astype(BF16)
                project(layer + 1, p, normed)
                send_kv(layer + 1, p)
                project_own(layer + 1, p, normed)

    for layer in range(LAYERS):
        for k in range(1, head_count):
            for n in range(len(chunks)):
                bias_copy(n, layer, k).wait_send()
            for p in range(len(gated_parts[layer])):
                gated_copy(layer, p, k).wait_send()
            out_copy(layer, k).wait_send()
            out_forward(layer, k).wait_send()
        for p in range(len(kv_parts[layer])):
            for d in range(chips):
                kv_forward(layer, p, d).wait_send()
                if d:
                    kv_copy(layer, p, d).wait_send()


def on_device(
    head_count, pb_count, pair, tokens, token_mask, w_gu, w_down, w_bias, w_q, w_k, w_v, w_gate, w_out
):
    rows, cols, channels = pair.shape
    width = w_q.shape[2]
    features = tokens.shape[1]
    local_heads = width // HD
    chips = pb_count // CORES
    chunks = len(pair_chunks(rows))
    parts = len(token_parts(rows))
    vmem = pl.BlockSpec(memory_space=pltpu.VMEM)
    anywhere = pl.BlockSpec(memory_space=pl.ANY)
    dma = pltpu.SemaphoreType.DMA
    bias_shape = (head_count, LAYERS, rows // ROW_TILE, local_heads, ROW_TILE, cols)
    return pl.pallas_call(
        functools.partial(step_kernel, head_count, pb_count),
        out_shape=jax.ShapeDtypeStruct((rows, features), BF16),
        in_specs=[anywhere] + [vmem] * 5 + [anywhere] * 5,
        out_specs=vmem,
        scratch_shapes=[
            pltpu.VMEM(pair.shape, BF16),
            pltpu.VMEM(w_gu.shape, BF16),
            pltpu.VMEM(w_down.shape, BF16),
            pltpu.VMEM((LAYERS, 4 * width, features), BF16),
            pltpu.VMEM((LAYERS, head_count, CORES, width // CORES, features), BF16),
            pltpu.VMEM(bias_shape, BF16),
            pltpu.VMEM(bias_shape, BF16),
            pltpu.VMEM((LAYERS, pb_count, rows, 2 * width), BF16),
            pltpu.VMEM((rows, 2 * width), BF16),
            pltpu.VMEM((LAYERS, head_count, rows, width), BF16),
            pltpu.VMEM((rows, features), F32),
            dma((chunks,)),
            dma((LAYERS, 4 + CORES)),
            dma((chunks, LAYERS, head_count)),
            dma((chunks, LAYERS, head_count)),
            dma((LAYERS, parts, chips)),
            dma((LAYERS, parts, chips)),
            dma((LAYERS, parts, chips)),
            dma((LAYERS, parts, chips)),
            dma((LAYERS, parts, head_count)),
            dma((LAYERS, parts, head_count)),
            dma((LAYERS, head_count)),
            dma((LAYERS, head_count)),
            dma((LAYERS, head_count)),
            dma((LAYERS, head_count)),
        ],
        compiler_params=pltpu.CompilerParams(
            collective_id=0, has_side_effects=True, vmem_limit_bytes=60 * 1024 * 1024
        ),
        name="diffusion_step",
    )(
        pair,
        tokens,
        token_mask.reshape(1, -1),
        w_gu,
        w_down,
        w_bias.T,
        jnp.swapaxes(w_q, 1, 2),
        jnp.swapaxes(w_k, 1, 2),
        jnp.swapaxes(w_v, 1, 2),
        jnp.swapaxes(w_gate, 1, 2),
        w_out,
    )


def solution(mesh):
    placed = (
        P("pb", "head", None),
        P("pb", None),
        P(),
        P(),
        P(),
        P(),
        P(None, None, "head"),
        P(None, None, "head"),
        P(None, None, "head"),
        P(None, None, "head"),
        P(None, "head", None),
    )
    return jax.shard_map(
        functools.partial(on_device, mesh.shape["head"], mesh.shape["pb"]),
        mesh=mesh,
        in_specs=placed,
        out_specs=P("pb", None),
        check_vma=False,
    )
```

```python
import functools

import jax
import jax.numpy as jnp
from jax import lax
from jax.experimental import pallas as pl
from jax.experimental.pallas import tpu as pltpu
from jax.sharding import PartitionSpec as P

TRANS = 2
LAYERS = 2
HD = 48
CORES = 2
ROW_TILE = 16
GROUP = 8
LANES = 128
F32 = jnp.float32
BF16 = jnp.bfloat16


def normalize(values):
    inverse = 1.0 / values.shape[-1]
    center = values - jnp.sum(values, axis=-1, keepdims=True) * inverse
    spread = jnp.sum(center * center, axis=-1, keepdims=True) * inverse
    return center * lax.rsqrt(spread + 1e-05)


def scale_rows(center):
    inverse = 1.0 / center.shape[-1]
    spread = jnp.sum(center * center, axis=-1, keepdims=True) * inverse
    return (center * lax.rsqrt(spread + 1e-05)).astype(BF16)


def matmul(left, right):
    return jnp.dot(left, right, preferred_element_type=F32)


def matmul_t(left, right):
    return lax.dot_general(left, right, (((1,), (1,)), ((), ())), preferred_element_type=F32)


def pair_chunks(rows):
    tiles = rows // ROW_TILE
    counts = [1, tiles - 2, 1] if tiles > 2 else [1] * tiles
    starts = [sum(counts[:n]) for n in range(len(counts))]
    return [(a * ROW_TILE, c * ROW_TILE) for a, c in zip(starts, counts)]


def token_parts(rows):
    last = pair_chunks(rows)[-1][0]
    return [(0, last), (last, rows - last)]


def step_kernel(
    head_count,
    pb_count,
    pair_hbm,
    tokens_hbm,
    mask_hbm,
    gu_hbm,
    down_hbm,
    bias_w_hbm,
    q_hbm,
    k_hbm,
    v_hbm,
    gate_hbm,
    out_hbm,
    result_ref,
    tokens_ref,
    mask_ref,
    gu_ref,
    down_ref,
    bias_w_ref,
    pair_v,
    gu_v,
    down_v,
    wide_w,
    out_w,
    bias_out,
    bias_in,
    kv_all,
    query_gate,
    gated_all,
    state_v,
    small_sem,
    pair_sem,
    weight_sem,
    bias_send,
    bias_recv,
    kv_send,
    kv_recv,
    fwd_send,
    fwd_recv,
    gated_send,
    gated_recv,
    out_send,
    out_recv,
    out_fwd_send,
    out_fwd_recv,
):
    rows, cols, channels = pair_hbm.shape
    width = q_hbm.shape[1]
    features = tokens_hbm.shape[1]
    local_heads = width // HD
    heads_all = local_heads * head_count
    half_width = width // CORES
    chips = pb_count // CORES
    col_blocks = cols // LANES
    hidden = down_hbm.shape[1]
    chunks = pair_chunks(rows)
    parts = token_parts(rows)
    kv_parts = [[(0, rows)]] + [parts] * (LAYERS - 1)
    gated_parts = [parts] * (LAYERS - 1) + [[(0, rows)]]

    head = lax.axis_index("head")
    pb = lax.axis_index("pb")
    core = lax.rem(pb, CORES)
    chip = pb // CORES
    partner = chip * CORES + (1 - core)

    def head_peer(k):
        return lax.rem(head + k, head_count)

    def chip_peer(d):
        return lax.rem(chip + d, chips) * CORES + core

    def chip_source(d):
        return lax.rem(chip + chips - d, chips) * CORES + core

    def projection_copies(layer):
        return [
            pltpu.make_async_copy(
                source.at[layer],
                wide_w.at[layer, index * width : (index + 1) * width],
                weight_sem.at[layer, index],
            )
            for index, source in enumerate((k_hbm, v_hbm, q_hbm, gate_hbm))
        ]

    def own_out_copies(layer):
        return [
            pltpu.make_async_copy(
                out_hbm.at[layer, part * half_width : (part + 1) * half_width],
                out_w.at[layer, head, part],
                weight_sem.at[layer, 4 + part],
            )
            for part in range(CORES)
        ]

    def pair_copy(n):
        first, count = chunks[n]
        return pltpu.make_async_copy(
            pair_hbm.at[first : first + count], pair_v.at[first : first + count], pair_sem.at[n]
        )

    small = ((gu_hbm, gu_ref), (down_hbm, down_ref), (bias_w_hbm, bias_w_ref))
    small += ((tokens_hbm, tokens_ref), (mask_hbm, mask_ref))
    small_copies = [
        pltpu.make_async_copy(source, target, small_sem.at[n])
        for n, (source, target) in enumerate(small)
    ]
    pair_copy(0).start()
    for copy in small_copies[:3]:
        copy.start()
    barrier = pltpu.get_barrier_semaphore()
    for k in range(1, head_count):
        pl.semaphore_signal(
            barrier, inc=1, device_id=(head_peer(k), pb), device_id_type=pl.DeviceIdType.MESH
        )
    for d in range(1, chips):
        pl.semaphore_signal(
            barrier, inc=1, device_id=(head, chip_peer(d)), device_id_type=pl.DeviceIdType.MESH
        )
    pl.semaphore_signal(
        barrier, inc=1, device_id=(head, partner), device_id_type=pl.DeviceIdType.MESH
    )

    for copy in small_copies[3:] + projection_copies(0):
        copy.start()
    for n in range(1, len(chunks)):
        pair_copy(n).start()
    for layer in range(LAYERS):
        for copy in own_out_copies(layer) + (projection_copies(layer) if layer else []):
            copy.start()

    def remote(source, target, send, recv, where):
        return pltpu.make_async_remote_copy(
            src_ref=source,
            dst_ref=target,
            send_sem=send,
            recv_sem=recv,
            device_id=where,
            device_id_type=pl.DeviceIdType.MESH,
        )

    def span(part):
        return slice(part[0], part[0] + part[1])

    def kv_copy(layer, p, d):
        block = kv_all.at[layer, pb, span(kv_parts[layer][p])]
        return remote(
            block, block, kv_send.at[layer, p, d], kv_recv.at[layer, p, d], (head, chip_peer(d))
        )

    def kv_forward(layer, p, d):
        block = kv_all.at[layer, chip_source(d), span(kv_parts[layer][p])]
        return remote(
            block, block, fwd_send.at[layer, p, d], fwd_recv.at[layer, p, d], (head, partner)
        )

    def out_copy(layer, k):
        return remote(
            out_hbm.at[layer, pl.ds(pl.multiple_of(core * half_width, half_width), half_width)],
            out_w.at[layer, head, core],
            out_send.at[layer, k],
            out_recv.at[layer, k],
            (head_peer(k), pb),
        )

    def out_forward(layer, k):
        block = out_w.at[layer, lax.rem(head + head_count - k, head_count), core]
        return remote(
            block, block, out_fwd_send.at[layer, k], out_fwd_recv.at[layer, k], (head, partner)
        )

    def forward_out(layer):
        for k in range(1, head_count):
            out_copy(layer, k).wait_recv()
            out_forward(layer, k).start()

    def gated_copy(layer, p, k):
        block = gated_all.at[layer, head, span(gated_parts[layer][p])]
        return remote(
            block, block, gated_send.at[layer, p, k], gated_recv.at[layer, p, k], (head_peer(k), pb)
        )

    def bias_copy(n, layer, k):
        first, count = chunks[n]
        where = slice(first // ROW_TILE, (first + count) // ROW_TILE)
        return remote(
            bias_out.at[head_peer(k), layer, where],
            bias_in.at[head, layer, where],
            bias_send.at[n, layer, k],
            bias_recv.at[n, layer, k],
            (head_peer(k), pb),
        )

    def project(layer, p, normed):
        where = span(kv_parts[layer][p])
        kv_all[layer, pb, where] = matmul_t(normed, wide_w[layer, : 2 * width]).astype(BF16)

    def send_kv(layer, p):
        for d in range(1, chips):
            kv_copy(layer, p, d).start()
        kv_forward(layer, p, 0).start()

    def project_own(layer, p, normed):
        where = span(kv_parts[layer][p])
        query_gate[where] = matmul_t(normed, wide_w[layer, 2 * width :]).astype(BF16)

    def forward_kv(layer, p):
        for d in range(1, chips):
            kv_copy(layer, p, d).wait_recv()
            kv_forward(layer, p, d).start()

    def finish_kv(layer, p):
        for d in range(chips):
            kv_forward(layer, p, d).wait_recv()

    for copy in small_copies[:3]:
        copy.wait()
    for section in range(TRANS):
        gu_v[section, :, :hidden] = (gu_ref[section, :, :hidden].astype(F32) * 0.5).astype(BF16)
        gu_v[section, :, hidden:] = gu_ref[section, :, hidden:]
        down = down_ref[section].astype(F32)
        level = jnp.sum(down, axis=-1, keepdims=True) * (1.0 / channels)
        down_v[section] = (down - level).astype(BF16)
    bias_w = bias_w_ref[...]

    def pair_block(first_row, row_count, first_col):
        blocks = []
        for start in range(0, row_count, GROUP):
            count = min(GROUP, row_count - start)
            wide = (
                pair_v[pl.ds(first_row + start, count), pl.ds(first_col, LANES), :]
                .reshape(count * LANES, channels)
                .astype(F32)
            )
            blocks.append(wide - jnp.sum(wide, axis=-1, keepdims=True) * (1.0 / channels))
        for section in range(TRANS):
            for n, center in enumerate(blocks):
                mixed = matmul(scale_rows(center), gu_v[section])
                gate = mixed[:, :hidden]
                units = ((gate + gate * jnp.tanh(gate)) * mixed[:, hidden:]).astype(BF16)
                blocks[n] = center + matmul(units, down_v[section])
        planes = []
        for center in blocks:
            projected = matmul_t(bias_w, scale_rows(center))
            planes += [
                projected[:, i : i + LANES] for i in range(0, projected.shape[1], LANES)
            ]
        by_head = jnp.transpose(jnp.stack(planes, axis=0), (1, 0, 2)).astype(BF16)
        for layer in range(LAYERS):
            for target in range(head_count):
                start = layer * heads_all + target * local_heads
                for row in range(0, row_count, ROW_TILE):
                    tile = (first_row + row) // ROW_TILE
                    bias_out[target, layer, tile, :, :, pl.ds(first_col, LANES)] = by_head[
                        start : start + local_heads, row : row + ROW_TILE
                    ]
        tiles = slice(first_row // ROW_TILE, (first_row + row_count) // ROW_TILE)
        bias_in[head, :, tiles, :, :, pl.ds(first_col, LANES)] = bias_out[
            head, :, tiles, :, :, pl.ds(first_col, LANES)
        ]

    def pair_step(n):
        pair_copy(n).wait()
        first_row, row_count = chunks[n]
        if col_blocks == 1:
            pair_block(first_row, row_count, 0)
        else:

            def one(block, carry):
                pair_block(first_row, row_count, pl.multiple_of(block * LANES, LANES))
                return carry

            lax.fori_loop(0, col_blocks, one, 0)

    def send_bias(n, layer):
        for k in range(1, head_count):
            bias_copy(n, layer, k).start()

    def wait_bias(layer, part):
        for n, (first, count) in enumerate(chunks):
            if part[0] <= first < part[0] + part[1]:
                for k in range(1, head_count):
                    bias_copy(n, layer, k).wait_recv()

    pair_step(0)
    for copy in small_copies[3:] + projection_copies(0):
        copy.wait()
    normed = normalize(tokens_ref[...].astype(F32)).astype(BF16)
    project(0, 0, normed)
    pl.semaphore_wait(barrier, head_count + chips - 1)
    send_kv(0, 0)
    send_bias(0, 0)
    for k in range(1, head_count):
        out_copy(0, k).start()
    project_own(0, 0, normed)
    for n in range(1, len(chunks)):
        if n == len(chunks) - 1:
            forward_kv(0, 0)
        pair_step(n)
        send_bias(n, 0)
    if len(chunks) == 1:
        forward_kv(0, 0)

    mask_row = mask_ref[...]
    real_count = jnp.sum(mask_row.astype(F32), axis=1, keepdims=True)
    is_real = mask_row == 1
    row_index = (lax.broadcasted_iota(jnp.int32, (rows, 1), 0) + pb * rows).astype(F32)
    row_real = (row_index < real_count).astype(F32)
    scale = 1.0 / HD**0.5

    def attend(layer, part):
        first, count = part
        keys_values = kv_all[layer].reshape(pb_count * rows, 2 * width)
        queries = query_gate[span(part)]
        lane = lax.broadcasted_iota(jnp.int32, (ROW_TILE, 2 * width), 1)
        tiles = range(0, count, ROW_TILE)
        spread_q = jnp.concatenate(
            [
                jnp.where(
                    (lane >= h * HD) & (lane < (h + 1) * HD), queries[t : t + ROW_TILE], jnp.zeros((), BF16)
                )
                for t in tiles
                for h in range(local_heads)
            ],
            axis=0,
        )
        scores = matmul_t(spread_q, keys_values) * scale
        wait_bias(layer, part)
        bias = jnp.concatenate(
            [
                bias_in[
                    source, layer, first // ROW_TILE : (first + count) // ROW_TILE
                ].reshape(local_heads * count, cols)
                for source in range(head_count)
            ],
            axis=1,
        )
        scores = scores + bias.astype(F32)
        scores = jnp.where(is_real, scores, -1e30)
        peak = jnp.max(scores, axis=1, keepdims=True)
        weights = jnp.exp(scores - peak)
        total = jnp.sum(weights, axis=1, keepdims=True)
        mixed = matmul(weights.astype(BF16), keys_values) / total
        rows_of = []
        for t in tiles:
            attended = jnp.zeros((ROW_TILE, 2 * width), F32)
            for h in range(local_heads):
                keep = (lane >= width + h * HD) & (lane < width + (h + 1) * HD)
                start = t * local_heads + h * ROW_TILE
                attended = attended + jnp.where(keep, mixed[start : start + ROW_TILE], 0.0)
            rows_of.append(attended)
        attended = jnp.concatenate(rows_of, axis=0)
        gated = (attended * jax.nn.sigmoid(queries.astype(F32))).astype(BF16)
        gated_all[layer, head, span(part)] = gated[:, width:]

    state_v[...] = tokens_ref[...].astype(F32)
    for layer in range(LAYERS):
        if layer:
            for p in range(len(kv_parts[layer])):
                forward_kv(layer, p)
        for p in range(len(kv_parts[layer])):
            finish_kv(layer, p)
        for p, part in enumerate(gated_parts[layer]):
            attend(layer, part)
            for k in range(1, head_count):
                gated_copy(layer, p, k).start()
            if not p:
                forward_out(layer)
        if layer + 1 < LAYERS:
            for n in range(len(chunks)):
                send_bias(n, layer + 1)
            for k in range(1, head_count):
                out_copy(layer + 1, k).start()
        for k in range(1, head_count):
            out_forward(layer, k).wait_recv()
        for copy in own_out_copies(layer):
            copy.wait()
        last = layer == LAYERS - 1
        for p, part in enumerate([(0, rows)] if last else gated_parts[layer]):
            where = span(part)
            for q in range(len(gated_parts[layer])) if last else (p,):
                for k in range(1, head_count):
                    gated_copy(layer, q, k).wait_recv()
            gathered = jnp.concatenate(
                [gated_all[layer, h, where] for h in range(head_count)], axis=1
            )
            update = matmul(gathered, out_w[layer].reshape(head_count * width, features))
            state = state_v[where] + row_real[where] * update
            if last:
                result_ref[where] = state.astype(BF16)
            else:
                if not p:
                    for copy in projection_copies(layer + 1):
                        copy.wait()
                state_v[where] = state
                normed = normalize(state).astype(BF16)
                project(layer + 1, p, normed)
                send_kv(layer + 1, p)
                project_own(layer + 1, p, normed)

    for layer in range(LAYERS):
        for k in range(1, head_count):
            for n in range(len(chunks)):
                bias_copy(n, layer, k).wait_send()
            for p in range(len(gated_parts[layer])):
                gated_copy(layer, p, k).wait_send()
            out_copy(layer, k).wait_send()
            out_forward(layer, k).wait_send()
        for p in range(len(kv_parts[layer])):
            for d in range(chips):
                kv_forward(layer, p, d).wait_send()
                if d:
                    kv_copy(layer, p, d).wait_send()


def on_device(
    head_count, pb_count, pair, tokens, token_mask, w_gu, w_down, w_bias, w_q, w_k, w_v, w_gate, w_out
):
    rows, cols, channels = pair.shape
    width = w_q.shape[2]
    features = tokens.shape[1]
    local_heads = width // HD
    chips = pb_count // CORES
    chunks = len(pair_chunks(rows))
    parts = len(token_parts(rows))
    vmem = pl.BlockSpec(memory_space=pltpu.VMEM)
    anywhere = pl.BlockSpec(memory_space=pl.ANY)
    dma = pltpu.SemaphoreType.DMA
    bias_shape = (head_count, LAYERS, rows // ROW_TILE, local_heads, ROW_TILE, cols)
    return pl.pallas_call(
        functools.partial(step_kernel, head_count, pb_count),
        out_shape=pltpu.VMEM((rows, features), BF16),
        in_specs=[anywhere] * 11,
        out_specs=vmem,
        scratch_shapes=[
            pltpu.VMEM(tokens.shape, BF16),
            pltpu.VMEM((1, token_mask.shape[0]), jnp.int32),
            pltpu.VMEM(w_gu.shape, BF16),
            pltpu.VMEM(w_down.shape, BF16),
            pltpu.VMEM(w_bias.shape[::-1], BF16),
            pltpu.VMEM(pair.shape, BF16),
            pltpu.VMEM(w_gu.shape, BF16),
            pltpu.VMEM(w_down.shape, BF16),
            pltpu.VMEM((LAYERS, 4 * width, features), BF16),
            pltpu.VMEM((LAYERS, head_count, CORES, width // CORES, features), BF16),
            pltpu.VMEM(bias_shape, BF16),
            pltpu.VMEM(bias_shape, BF16),
            pltpu.VMEM((LAYERS, pb_count, rows, 2 * width), BF16),
            pltpu.VMEM((rows, 2 * width), BF16),
            pltpu.VMEM((LAYERS, head_count, rows, width), BF16),
            pltpu.VMEM((rows, features), F32),
            dma((5,)),
            dma((chunks,)),
            dma((LAYERS, 4 + CORES)),
            dma((chunks, LAYERS, head_count)),
            dma((chunks, LAYERS, head_count)),
            dma((LAYERS, parts, chips)),
            dma((LAYERS, parts, chips)),
            dma((LAYERS, parts, chips)),
            dma((LAYERS, parts, chips)),
            dma((LAYERS, parts, head_count)),
            dma((LAYERS, parts, head_count)),
            dma((LAYERS, head_count)),
            dma((LAYERS, head_count)),
            dma((LAYERS, head_count)),
            dma((LAYERS, head_count)),
        ],
        compiler_params=pltpu.CompilerParams(
            collective_id=0, has_side_effects=True, vmem_limit_bytes=60 * 1024 * 1024
        ),
        name="diffusion_step",
    )(
        pair,
        tokens,
        token_mask.reshape(1, -1),
        w_gu,
        w_down,
        w_bias.T,
        jnp.swapaxes(w_q, 1, 2),
        jnp.swapaxes(w_k, 1, 2),
        jnp.swapaxes(w_v, 1, 2),
        jnp.swapaxes(w_gate, 1, 2),
        w_out,
    )


def solution(mesh):
    placed = (
        P("pb", "head", None),
        P("pb", None),
        P(),
        P(),
        P(),
        P(),
        P(None, None, "head"),
        P(None, None, "head"),
        P(None, None, "head"),
        P(None, None, "head"),
        P(None, "head", None),
    )
    return jax.shard_map(
        functools.partial(on_device, mesh.shape["head"], mesh.shape["pb"]),
        mesh=mesh,
        in_specs=placed,
        out_specs=P("pb", None),
        check_vma=False,
    )
```

```python
import functools

import jax
import jax.numpy as jnp
from jax import lax
from jax.experimental import pallas as pl
from jax.experimental.pallas import tpu as pltpu
from jax.sharding import PartitionSpec as P

TRANS = 2
LAYERS = 2
HD = 48
CORES = 2
ROW_TILE = 16
GROUP = 8
LANES = 128
F32 = jnp.float32
BF16 = jnp.bfloat16


def normalize(values):
    inverse = 1.0 / values.shape[-1]
    center = values - jnp.sum(values, axis=-1, keepdims=True) * inverse
    spread = jnp.sum(center * center, axis=-1, keepdims=True) * inverse
    return center * lax.rsqrt(spread + 1e-05)


def scale_rows(center):
    inverse = 1.0 / center.shape[-1]
    spread = jnp.sum(center * center, axis=-1, keepdims=True) * inverse
    return (center * lax.rsqrt(spread + 1e-05)).astype(BF16)


def matmul(left, right):
    return jnp.dot(left, right, preferred_element_type=F32)


def matmul_t(left, right):
    return lax.dot_general(left, right, (((1,), (1,)), ((), ())), preferred_element_type=F32)


def pair_chunks(rows):
    tiles = rows // ROW_TILE
    counts = [1, tiles - 2, 1] if tiles > 2 else [1] * tiles
    starts = [sum(counts[:n]) for n in range(len(counts))]
    return [(a * ROW_TILE, c * ROW_TILE) for a, c in zip(starts, counts)]


def token_parts(rows):
    last = pair_chunks(rows)[-1][0]
    return [(0, last), (last, rows - last)]


def step_kernel(
    head_count,
    pb_count,
    pair_hbm,
    tokens_hbm,
    mask_hbm,
    gu_hbm,
    down_hbm,
    bias_w_hbm,
    q_hbm,
    k_hbm,
    v_hbm,
    gate_hbm,
    out_hbm,
    result_ref,
    tokens_ref,
    mask_ref,
    gu_ref,
    down_ref,
    bias_w_ref,
    pair_v,
    gu_v,
    down_v,
    wide_w,
    out_w,
    bias_out,
    bias_in,
    kv_all,
    query_gate,
    gated_all,
    state_v,
    small_sem,
    pair_sem,
    weight_sem,
    bias_send,
    bias_recv,
    kv_send,
    kv_recv,
    fwd_send,
    fwd_recv,
    gated_send,
    gated_recv,
    out_send,
    out_recv,
    out_fwd_send,
    out_fwd_recv,
):
    rows, cols, channels = pair_hbm.shape
    width = q_hbm.shape[1]
    features = tokens_hbm.shape[1]
    local_heads = width // HD
    heads_all = local_heads * head_count
    half_width = width // CORES
    chips = pb_count // CORES
    col_blocks = cols // LANES
    hidden = down_hbm.shape[1]
    chunks = pair_chunks(rows)
    parts = token_parts(rows)
    kv_parts = [[(0, rows)]] + [parts] * (LAYERS - 1)
    gated_parts = [parts] * (LAYERS - 1) + [[(0, rows)]]

    head = lax.axis_index("head")
    pb = lax.axis_index("pb")
    core = lax.rem(pb, CORES)
    chip = pb // CORES
    partner = chip * CORES + (1 - core)

    def head_peer(k):
        return lax.rem(head + k, head_count)

    def chip_peer(d):
        return lax.rem(chip + d, chips) * CORES + core

    def chip_source(d):
        return lax.rem(chip + chips - d, chips) * CORES + core

    def projection_copies(layer):
        return [
            pltpu.make_async_copy(
                source.at[layer],
                wide_w.at[layer, index * width : (index + 1) * width],
                weight_sem.at[layer, index],
            )
            for index, source in enumerate((k_hbm, v_hbm, q_hbm, gate_hbm))
        ]

    def own_out_copies(layer):
        return [
            pltpu.make_async_copy(
                out_hbm.at[layer, part * half_width : (part + 1) * half_width],
                out_w.at[layer, head, part],
                weight_sem.at[layer, 4 + part],
            )
            for part in range(CORES)
        ]

    def pair_copy(n):
        first, count = chunks[n]
        return pltpu.make_async_copy(
            pair_hbm.at[first : first + count], pair_v.at[first : first + count], pair_sem.at[n]
        )

    small = ((gu_hbm, gu_ref), (down_hbm, down_ref), (bias_w_hbm, bias_w_ref))
    small += ((tokens_hbm, tokens_ref), (mask_hbm, mask_ref))
    small_copies = [
        pltpu.make_async_copy(source, target, small_sem.at[n])
        for n, (source, target) in enumerate(small)
    ]
    pair_copy(0).start()
    for copy in small_copies[:3]:
        copy.start()
    barrier = pltpu.get_barrier_semaphore()
    for k in range(1, head_count):
        pl.semaphore_signal(
            barrier, inc=1, device_id=(head_peer(k), pb), device_id_type=pl.DeviceIdType.MESH
        )
    for d in range(1, chips):
        pl.semaphore_signal(
            barrier, inc=1, device_id=(head, chip_peer(d)), device_id_type=pl.DeviceIdType.MESH
        )
    pl.semaphore_signal(
        barrier, inc=1, device_id=(head, partner), device_id_type=pl.DeviceIdType.MESH
    )

    for copy in small_copies[3:] + projection_copies(0):
        copy.start()
    for n in range(1, len(chunks)):
        pair_copy(n).start()
    for layer in range(LAYERS):
        for copy in own_out_copies(layer) + (projection_copies(layer) if layer else []):
            copy.start()

    def remote(source, target, send, recv, where):
        return pltpu.make_async_remote_copy(
            src_ref=source,
            dst_ref=target,
            send_sem=send,
            recv_sem=recv,
            device_id=where,
            device_id_type=pl.DeviceIdType.MESH,
        )

    def span(part):
        return slice(part[0], part[0] + part[1])

    def kv_index(layer, p):
        return sum(len(each) for each in kv_parts[:layer]) + p

    def gated_index(layer, p):
        return sum(len(each) for each in gated_parts[:layer]) + p

    def wait_bytes(block, semaphore):
        pltpu.make_async_copy(block, block, semaphore).wait()

    def kv_copy(layer, p, d):
        block = kv_all.at[layer, pb, span(kv_parts[layer][p])]
        return remote(
            block, block, kv_send.at[layer], kv_recv.at[kv_index(layer, p), d - 1], (head, chip_peer(d))
        )

    def kv_forward(layer, p, d):
        block = kv_all.at[layer, chip_source(d), span(kv_parts[layer][p])]
        return remote(
            block, block, fwd_send.at[layer], fwd_recv.at[kv_index(layer, p)], (head, partner)
        )

    def out_copy(layer, k):
        return remote(
            out_hbm.at[layer, pl.ds(pl.multiple_of(core * half_width, half_width), half_width)],
            out_w.at[layer, head, core],
            out_send.at[layer],
            out_recv.at[layer],
            (head_peer(k), pb),
        )

    def out_forward(layer, k):
        block = out_w.at[layer, lax.rem(head + head_count - k, head_count), core]
        return remote(
            block, block, out_fwd_send.at[layer], out_fwd_recv.at[layer], (head, partner)
        )

    def forward_out(layer):
        wait_bytes(out_w.at[layer, 1:head_count, 0], out_recv.at[layer])
        for k in range(1, head_count):
            out_forward(layer, k).start()

    def gated_copy(layer, p, k):
        block = gated_all.at[layer, head, span(gated_parts[layer][p])]
        return remote(
            block,
            block,
            gated_send.at[layer],
            gated_recv.at[gated_index(layer, p)],
            (head_peer(k), pb),
        )

    def bias_copy(n, layer, k):
        first, count = chunks[n]
        where = slice(first // ROW_TILE, (first + count) // ROW_TILE)
        return remote(
            bias_out.at[head_peer(k), layer, where],
            bias_in.at[head, layer, where],
            bias_send.at[layer],
            bias_recv.at[n, layer],
            (head_peer(k), pb),
        )

    def project(layer, p, normed):
        where = span(kv_parts[layer][p])
        kv_all[layer, pb, where] = matmul_t(normed, wide_w[layer, : 2 * width]).astype(BF16)

    def send_kv(layer, p):
        for d in range(1, chips):
            kv_copy(layer, p, d).start()
        kv_forward(layer, p, 0).start()

    def project_own(layer, p, normed):
        where = span(kv_parts[layer][p])
        query_gate[where] = matmul_t(normed, wide_w[layer, 2 * width :]).astype(BF16)

    def forward_kv(layer, p):
        for d in range(1, chips):
            kv_copy(layer, p, d).wait_recv()
            kv_forward(layer, p, d).start()

    def finish_kv(layer, p):
        wait_bytes(
            kv_all.at[layer, :chips, span(kv_parts[layer][p])], fwd_recv.at[kv_index(layer, p)]
        )

    for copy in small_copies[:3]:
        copy.wait()
    for section in range(TRANS):
        gu_v[section, :, :hidden] = (gu_ref[section, :, :hidden].astype(F32) * 0.5).astype(BF16)
        gu_v[section, :, hidden:] = gu_ref[section, :, hidden:]
        down = down_ref[section].astype(F32)
        level = jnp.sum(down, axis=-1, keepdims=True) * (1.0 / channels)
        down_v[section] = (down - level).astype(BF16)
    bias_w = bias_w_ref[...]
    square = (channels, channels)
    diagonal = lax.broadcasted_iota(jnp.int32, square, 0) == lax.broadcasted_iota(jnp.int32, square, 1)
    centring = (jnp.where(diagonal, 1.0, 0.0) - 1.0 / channels).astype(BF16)

    def pair_block(first_row, row_count, first_col):
        blocks = []
        for start in range(0, row_count, GROUP):
            count = min(GROUP, row_count - start)
            block = pair_v[pl.ds(first_row + start, count), pl.ds(first_col, LANES), :]
            blocks.append(matmul(block.reshape(count * LANES, channels), centring))
        for section in range(TRANS):
            for n, center in enumerate(blocks):
                mixed = matmul(scale_rows(center), gu_v[section])
                gate = mixed[:, :hidden]
                units = ((gate + gate * jnp.tanh(gate)) * mixed[:, hidden:]).astype(BF16)
                blocks[n] = center + matmul(units, down_v[section])
        planes = []
        for center in blocks:
            projected = matmul_t(bias_w, scale_rows(center))
            planes += [
                projected[:, i : i + LANES] for i in range(0, projected.shape[1], LANES)
            ]
        by_head = jnp.transpose(jnp.stack(planes, axis=0), (1, 0, 2)).astype(BF16)
        for layer in range(LAYERS):
            for target in range(head_count):
                start = layer * heads_all + target * local_heads
                for row in range(0, row_count, ROW_TILE):
                    tile = (first_row + row) // ROW_TILE
                    bias_out[target, layer, tile, :, :, pl.ds(first_col, LANES)] = by_head[
                        start : start + local_heads, row : row + ROW_TILE
                    ]
        tiles = slice(first_row // ROW_TILE, (first_row + row_count) // ROW_TILE)
        bias_in[head, :, tiles, :, :, pl.ds(first_col, LANES)] = bias_out[
            head, :, tiles, :, :, pl.ds(first_col, LANES)
        ]

    def pair_step(n):
        pair_copy(n).wait()
        first_row, row_count = chunks[n]
        if col_blocks == 1:
            pair_block(first_row, row_count, 0)
        else:

            def one(block, carry):
                pair_block(first_row, row_count, pl.multiple_of(block * LANES, LANES))
                return carry

            lax.fori_loop(0, col_blocks, one, 0)

    def send_bias(n, layer):
        for k in range(1, head_count):
            bias_copy(n, layer, k).start()

    def wait_bias(layer, part):
        for n, (first, count) in enumerate(chunks):
            if part[0] <= first < part[0] + part[1]:
                tiles = slice(first // ROW_TILE, (first + count) // ROW_TILE)
                wait_bytes(bias_in.at[1:head_count, layer, tiles], bias_recv.at[n, layer])

    pair_step(0)
    for copy in small_copies[3:] + projection_copies(0):
        copy.wait()
    normed = normalize(tokens_ref[...].astype(F32)).astype(BF16)
    project(0, 0, normed)
    pl.semaphore_wait(barrier, head_count + chips - 1)
    send_kv(0, 0)
    send_bias(0, 0)
    for k in range(1, head_count):
        out_copy(0, k).start()
    project_own(0, 0, normed)
    for n in range(1, len(chunks)):
        if n == len(chunks) - 1:
            forward_kv(0, 0)
        pair_step(n)
        send_bias(n, 0)
    if len(chunks) == 1:
        forward_kv(0, 0)

    mask_row = mask_ref[...]
    real_count = jnp.sum(mask_row.astype(F32), axis=1, keepdims=True)
    is_real = mask_row == 1
    row_index = (lax.broadcasted_iota(jnp.int32, (rows, 1), 0) + pb * rows).astype(F32)
    row_real = (row_index < real_count).astype(F32)
    scale = 1.0 / HD**0.5

    def attend(layer, part):
        first, count = part
        keys_values = kv_all[layer].reshape(pb_count * rows, 2 * width)
        queries = query_gate[span(part)]
        lane = lax.broadcasted_iota(jnp.int32, (ROW_TILE, 2 * width), 1)
        tiles = range(0, count, ROW_TILE)
        spread_q = jnp.concatenate(
            [
                jnp.where(
                    (lane >= h * HD) & (lane < (h + 1) * HD), queries[t : t + ROW_TILE], jnp.zeros((), BF16)
                )
                for t in tiles
                for h in range(local_heads)
            ],
            axis=0,
        )
        scores = matmul_t(spread_q, keys_values) * scale
        wait_bias(layer, part)
        bias = jnp.concatenate(
            [
                bias_in[
                    source, layer, first // ROW_TILE : (first + count) // ROW_TILE
                ].reshape(local_heads * count, cols)
                for source in range(head_count)
            ],
            axis=1,
        )
        scores = scores + bias.astype(F32)
        scores = jnp.where(is_real, scores, -1e30)
        peak = jnp.max(scores, axis=1, keepdims=True)
        weights = jnp.exp(scores - peak)
        total = jnp.sum(weights, axis=1, keepdims=True)
        mixed = matmul(weights.astype(BF16), keys_values) / total
        rows_of = []
        for t in tiles:
            attended = jnp.zeros((ROW_TILE, 2 * width), F32)
            for h in range(local_heads):
                keep = (lane >= width + h * HD) & (lane < width + (h + 1) * HD)
                start = t * local_heads + h * ROW_TILE
                attended = attended + jnp.where(keep, mixed[start : start + ROW_TILE], 0.0)
            rows_of.append(attended)
        attended = jnp.concatenate(rows_of, axis=0)
        gated = (attended * jax.nn.sigmoid(queries.astype(F32))).astype(BF16)
        gated_all[layer, head, span(part)] = gated[:, width:]

    state_v[...] = tokens_ref[...].astype(F32)
    for layer in range(LAYERS):
        if layer:
            for p in range(len(kv_parts[layer])):
                forward_kv(layer, p)
        for p in range(len(kv_parts[layer])):
            finish_kv(layer, p)
        for p, part in enumerate(gated_parts[layer]):
            attend(layer, part)
            for k in range(1, head_count):
                gated_copy(layer, p, k).start()
            if not p:
                forward_out(layer)
        if layer + 1 < LAYERS:
            for n in range(len(chunks)):
                send_bias(n, layer + 1)
            for k in range(1, head_count):
                out_copy(layer + 1, k).start()
        wait_bytes(out_w.at[layer, 1:head_count, 0], out_fwd_recv.at[layer])
        for copy in own_out_copies(layer):
            copy.wait()
        last = layer == LAYERS - 1
        for p, part in enumerate([(0, rows)] if last else gated_parts[layer]):
            where = span(part)
            for q in range(len(gated_parts[layer])) if last else (p,):
                wait_bytes(
                    gated_all.at[layer, 1:head_count, span(gated_parts[layer][q])],
                    gated_recv.at[gated_index(layer, q)],
                )
            gathered = jnp.concatenate(
                [gated_all[layer, h, where] for h in range(head_count)], axis=1
            )
            update = matmul(gathered, out_w[layer].reshape(head_count * width, features))
            state = state_v[where] + row_real[where] * update
            if last:
                result_ref[where] = state.astype(BF16)
            else:
                if not p:
                    for copy in projection_copies(layer + 1):
                        copy.wait()
                state_v[where] = state
                normed = normalize(state).astype(BF16)
                project(layer + 1, p, normed)
                send_kv(layer + 1, p)
                project_own(layer + 1, p, normed)

    for layer in range(LAYERS):
        wait_bytes(bias_out.at[1:head_count, layer], bias_send.at[layer])
        wait_bytes(gated_all.at[layer, 1:head_count], gated_send.at[layer])
        wait_bytes(out_w.at[layer, 1:head_count, 0], out_send.at[layer])
        wait_bytes(out_w.at[layer, 1:head_count, 0], out_fwd_send.at[layer])
        wait_bytes(kv_all.at[layer, 1:chips], kv_send.at[layer])
        wait_bytes(kv_all.at[layer, :chips], fwd_send.at[layer])


def on_device(
    head_count, pb_count, pair, tokens, token_mask, w_gu, w_down, w_bias, w_q, w_k, w_v, w_gate, w_out
):
    rows, cols, channels = pair.shape
    width = w_q.shape[2]
    features = tokens.shape[1]
    local_heads = width // HD
    chips = pb_count // CORES
    chunks = len(pair_chunks(rows))
    kv_parts = 1 + (LAYERS - 1) * len(token_parts(rows))
    vmem = pl.BlockSpec(memory_space=pltpu.VMEM)
    anywhere = pl.BlockSpec(memory_space=pl.ANY)
    dma = pltpu.SemaphoreType.DMA
    bias_shape = (head_count, LAYERS, rows // ROW_TILE, local_heads, ROW_TILE, cols)
    return pl.pallas_call(
        functools.partial(step_kernel, head_count, pb_count),
        out_shape=pltpu.VMEM((rows, features), BF16),
        in_specs=[anywhere] * 11,
        out_specs=vmem,
        scratch_shapes=[
            pltpu.VMEM(tokens.shape, BF16),
            pltpu.VMEM((1, token_mask.shape[0]), jnp.int32),
            pltpu.VMEM(w_gu.shape, BF16),
            pltpu.VMEM(w_down.shape, BF16),
            pltpu.VMEM(w_bias.shape[::-1], BF16),
            pltpu.VMEM(pair.shape, BF16),
            pltpu.VMEM(w_gu.shape, BF16),
            pltpu.VMEM(w_down.shape, BF16),
            pltpu.VMEM((LAYERS, 4 * width, features), BF16),
            pltpu.VMEM((LAYERS, head_count, CORES, width // CORES, features), BF16),
            pltpu.VMEM(bias_shape, BF16),
            pltpu.VMEM(bias_shape, BF16),
            pltpu.VMEM((LAYERS, pb_count, rows, 2 * width), BF16),
            pltpu.VMEM((rows, 2 * width), BF16),
            pltpu.VMEM((LAYERS, head_count, rows, width), BF16),
            pltpu.VMEM((rows, features), F32),
            dma((5,)),
            dma((chunks,)),
            dma((LAYERS, 4 + CORES)),
            dma((LAYERS,)),
            dma((chunks, LAYERS)),
            dma((LAYERS,)),
            dma((kv_parts, chips - 1)),
            dma((LAYERS,)),
            dma((kv_parts,)),
            dma((LAYERS,)),
            dma((kv_parts,)),
            dma((LAYERS,)),
            dma((LAYERS,)),
            dma((LAYERS,)),
            dma((LAYERS,)),
        ],
        compiler_params=pltpu.CompilerParams(
            collective_id=0, has_side_effects=True, vmem_limit_bytes=60 * 1024 * 1024
        ),
        name="diffusion_step",
    )(
        pair,
        tokens,
        token_mask.reshape(1, -1),
        w_gu,
        w_down,
        w_bias.T,
        jnp.swapaxes(w_q, 1, 2),
        jnp.swapaxes(w_k, 1, 2),
        jnp.swapaxes(w_v, 1, 2),
        jnp.swapaxes(w_gate, 1, 2),
        w_out,
    )


def solution(mesh):
    placed = (
        P("pb", "head", None),
        P("pb", None),
        P(),
        P(),
        P(),
        P(),
        P(None, None, "head"),
        P(None, None, "head"),
        P(None, None, "head"),
        P(None, None, "head"),
        P(None, "head", None),
    )
    return jax.shard_map(
        functools.partial(on_device, mesh.shape["head"], mesh.shape["pb"]),
        mesh=mesh,
        in_specs=placed,
        out_specs=P("pb", None),
        check_vma=False,
    )
```

```python
import functools

import jax
import jax.numpy as jnp
from jax import lax
from jax.experimental import pallas as pl
from jax.experimental.pallas import tpu as pltpu
from jax.sharding import PartitionSpec as P

TRANS = 2
LAYERS = 2
HD = 48
CORES = 2
ROW_TILE = 16
GROUP = 8
LANES = 128
F32 = jnp.float32
BF16 = jnp.bfloat16


def normalize(values):
    inverse = 1.0 / values.shape[-1]
    center = values - jnp.sum(values, axis=-1, keepdims=True) * inverse
    spread = jnp.sum(center * center, axis=-1, keepdims=True) * inverse
    return center * lax.rsqrt(spread + 1e-05)


def scale_rows(center):
    inverse = 1.0 / center.shape[-1]
    spread = jnp.sum(center * center, axis=-1, keepdims=True) * inverse
    return (center * lax.rsqrt(spread + 1e-05)).astype(BF16)


def matmul(left, right):
    return jnp.dot(left, right, preferred_element_type=F32)


def matmul_t(left, right):
    return lax.dot_general(left, right, (((1,), (1,)), ((), ())), preferred_element_type=F32)


def pair_chunks(rows):
    tiles = rows // ROW_TILE
    counts = [1, tiles - 2, 1] if tiles > 2 else [1] * tiles
    starts = [sum(counts[:n]) for n in range(len(counts))]
    return [(a * ROW_TILE, c * ROW_TILE) for a, c in zip(starts, counts)]


def token_parts(rows):
    last = pair_chunks(rows)[-1][0]
    return [(0, last), (last, rows - last)]


def step_kernel(
    head_count,
    pb_count,
    pair_hbm,
    tokens_hbm,
    mask_hbm,
    gu_hbm,
    down_hbm,
    bias_w_hbm,
    q_hbm,
    k_hbm,
    v_hbm,
    gate_hbm,
    out_hbm,
    result_ref,
    tokens_ref,
    mask_ref,
    gu_ref,
    down_ref,
    bias_w_ref,
    pair_v,
    gu_v,
    down_v,
    wide_w,
    out_w,
    bias_out,
    bias_in,
    kv_all,
    query_gate,
    gated_all,
    state_v,
    small_sem,
    pair_sem,
    weight_sem,
    bias_send,
    bias_recv,
    kv_send,
    kv_recv,
    fwd_send,
    fwd_recv,
    gated_send,
    gated_recv,
    out_send,
    out_recv,
    out_fwd_send,
    out_fwd_recv,
):
    rows, cols, channels = pair_hbm.shape
    width = q_hbm.shape[1]
    features = tokens_hbm.shape[1]
    local_heads = width // HD
    heads_all = local_heads * head_count
    half_width = width // CORES
    chips = pb_count // CORES
    col_blocks = cols // LANES
    hidden = down_hbm.shape[1]
    chunks = pair_chunks(rows)
    parts = token_parts(rows)
    kv_parts = [[(0, rows)]] + [parts] * (LAYERS - 1)
    gated_parts = [parts] * (LAYERS - 1) + [[(0, rows)]]

    head = lax.axis_index("head")
    pb = lax.axis_index("pb")
    core = lax.rem(pb, CORES)
    chip = pb // CORES
    partner = chip * CORES + (1 - core)

    def head_peer(k):
        return lax.rem(head + k, head_count)

    def chip_peer(d):
        return lax.rem(chip + d, chips) * CORES + core

    def chip_source(d):
        return lax.rem(chip + chips - d, chips) * CORES + core

    def projection_copies(layer):
        return [
            pltpu.make_async_copy(
                source.at[layer],
                wide_w.at[layer, index * width : (index + 1) * width],
                weight_sem.at[layer, index],
            )
            for index, source in enumerate((k_hbm, v_hbm, q_hbm, gate_hbm))
        ]

    def own_out_copies(layer):
        return [
            pltpu.make_async_copy(
                out_hbm.at[layer, part * half_width : (part + 1) * half_width],
                out_w.at[layer, head, part],
                weight_sem.at[layer, 4 + part],
            )
            for part in range(CORES)
        ]

    def pair_copy(n):
        first, count = chunks[n]
        return pltpu.make_async_copy(
            pair_hbm.at[first : first + count], pair_v.at[first : first + count], pair_sem.at[n]
        )

    small = ((gu_hbm, gu_ref), (down_hbm, down_ref), (bias_w_hbm, bias_w_ref))
    small += ((tokens_hbm, tokens_ref), (mask_hbm, mask_ref))
    small_copies = [
        pltpu.make_async_copy(source, target, small_sem.at[n])
        for n, (source, target) in enumerate(small)
    ]
    for copy in small_copies[3:] + projection_copies(0) + [pair_copy(0)] + small_copies[:3]:
        copy.start()
    barrier = pltpu.get_barrier_semaphore()
    for k in range(1, head_count):
        pl.semaphore_signal(
            barrier, inc=1, device_id=(head_peer(k), pb), device_id_type=pl.DeviceIdType.MESH
        )
    for d in range(1, chips):
        pl.semaphore_signal(
            barrier, inc=1, device_id=(head, chip_peer(d)), device_id_type=pl.DeviceIdType.MESH
        )
    pl.semaphore_signal(
        barrier, inc=1, device_id=(head, partner), device_id_type=pl.DeviceIdType.MESH
    )

    for n in range(1, len(chunks)):
        pair_copy(n).start()
    for layer in range(LAYERS):
        for copy in own_out_copies(layer) + (projection_copies(layer) if layer else []):
            copy.start()

    def remote(source, target, send, recv, where):
        return pltpu.make_async_remote_copy(
            src_ref=source,
            dst_ref=target,
            send_sem=send,
            recv_sem=recv,
            device_id=where,
            device_id_type=pl.DeviceIdType.MESH,
        )

    def span(part):
        return slice(part[0], part[0] + part[1])

    def kv_index(layer, p):
        return sum(len(each) for each in kv_parts[:layer]) + p

    def gated_index(layer, p):
        return sum(len(each) for each in gated_parts[:layer]) + p

    def wait_bytes(block, semaphore):
        pltpu.make_async_copy(block, block, semaphore).wait()

    def kv_copy(layer, p, d):
        block = kv_all.at[layer, pb, span(kv_parts[layer][p])]
        return remote(
            block, block, kv_send.at[layer], kv_recv.at[kv_index(layer, p), d - 1], (head, chip_peer(d))
        )

    def kv_forward(layer, p, d):
        block = kv_all.at[layer, chip_source(d), span(kv_parts[layer][p])]
        return remote(
            block, block, fwd_send.at[layer], fwd_recv.at[kv_index(layer, p)], (head, partner)
        )

    def out_copy(layer, k):
        return remote(
            out_hbm.at[layer, pl.ds(pl.multiple_of(core * half_width, half_width), half_width)],
            out_w.at[layer, head, core],
            out_send.at[layer],
            out_recv.at[layer],
            (head_peer(k), pb),
        )

    def out_forward(layer, k):
        block = out_w.at[layer, lax.rem(head + head_count - k, head_count), core]
        return remote(
            block, block, out_fwd_send.at[layer], out_fwd_recv.at[layer], (head, partner)
        )

    def forward_out(layer):
        wait_bytes(out_w.at[layer, 1:head_count, 0], out_recv.at[layer])
        for k in range(1, head_count):
            out_forward(layer, k).start()

    def gated_copy(layer, p, k):
        block = gated_all.at[layer, head, span(gated_parts[layer][p])]
        return remote(
            block,
            block,
            gated_send.at[layer],
            gated_recv.at[gated_index(layer, p)],
            (head_peer(k), pb),
        )

    def bias_copy(n, layer, k):
        first, count = chunks[n]
        where = slice(first // ROW_TILE, (first + count) // ROW_TILE)
        return remote(
            bias_out.at[head_peer(k), layer, where],
            bias_in.at[head, layer, where],
            bias_send.at[layer],
            bias_recv.at[n, layer],
            (head_peer(k), pb),
        )

    def project(layer, p, normed):
        where = span(kv_parts[layer][p])
        kv_all[layer, pb, where] = matmul_t(normed, wide_w[layer, : 2 * width]).astype(BF16)

    def send_kv(layer, p):
        for d in range(1, chips):
            kv_copy(layer, p, d).start()
        kv_forward(layer, p, 0).start()

    def project_own(layer, p, normed):
        where = span(kv_parts[layer][p])
        query_gate[where] = matmul_t(normed, wide_w[layer, 2 * width :]).astype(BF16)

    def forward_kv(layer, p):
        for d in range(1, chips):
            kv_copy(layer, p, d).wait_recv()
            kv_forward(layer, p, d).start()

    def finish_kv(layer, p):
        wait_bytes(
            kv_all.at[layer, :chips, span(kv_parts[layer][p])], fwd_recv.at[kv_index(layer, p)]
        )

    def pair_block(first_row, row_count, first_col):
        blocks = []
        for start in range(0, row_count, GROUP):
            count = min(GROUP, row_count - start)
            block = pair_v[pl.ds(first_row + start, count), pl.ds(first_col, LANES), :]
            blocks.append(matmul(block.reshape(count * LANES, channels), centring))
        for section in range(TRANS):
            for n, center in enumerate(blocks):
                mixed = matmul(scale_rows(center), gu_v[section])
                gate = mixed[:, :hidden]
                units = ((gate + gate * jnp.tanh(gate)) * mixed[:, hidden:]).astype(BF16)
                blocks[n] = center + matmul(units, down_v[section])
        planes = []
        for center in blocks:
            projected = matmul_t(bias_w, scale_rows(center))
            planes += [
                projected[:, i : i + LANES] for i in range(0, projected.shape[1], LANES)
            ]
        by_head = jnp.transpose(jnp.stack(planes, axis=0), (1, 0, 2)).astype(BF16)
        for layer in range(LAYERS):
            for target in range(head_count):
                start = layer * heads_all + target * local_heads
                for row in range(0, row_count, ROW_TILE):
                    tile = (first_row + row) // ROW_TILE
                    bias_out[target, layer, tile, :, :, pl.ds(first_col, LANES)] = by_head[
                        start : start + local_heads, row : row + ROW_TILE
                    ]
        tiles = slice(first_row // ROW_TILE, (first_row + row_count) // ROW_TILE)
        bias_in[head, :, tiles, :, :, pl.ds(first_col, LANES)] = bias_out[
            head, :, tiles, :, :, pl.ds(first_col, LANES)
        ]

    def pair_step(n):
        pair_copy(n).wait()
        first_row, row_count = chunks[n]
        if col_blocks == 1:
            pair_block(first_row, row_count, 0)
        else:

            def one(block, carry):
                pair_block(first_row, row_count, pl.multiple_of(block * LANES, LANES))
                return carry

            lax.fori_loop(0, col_blocks, one, 0)

    def send_bias(n, layer):
        for k in range(1, head_count):
            bias_copy(n, layer, k).start()

    def wait_bias(layer, part):
        for n, (first, count) in enumerate(chunks):
            if part[0] <= first < part[0] + part[1]:
                tiles = slice(first // ROW_TILE, (first + count) // ROW_TILE)
                wait_bytes(bias_in.at[1:head_count, layer, tiles], bias_recv.at[n, layer])

    for copy in small_copies[3:] + projection_copies(0):
        copy.wait()
    normed = normalize(tokens_ref[...].astype(F32)).astype(BF16)
    project(0, 0, normed)
    project_own(0, 0, normed)
    pl.semaphore_wait(barrier, head_count + chips - 1)
    send_kv(0, 0)
    for k in range(1, head_count):
        out_copy(0, k).start()
    for copy in small_copies[:3]:
        copy.wait()
    for section in range(TRANS):
        gu_v[section, :, :hidden] = (gu_ref[section, :, :hidden].astype(F32) * 0.5).astype(BF16)
        gu_v[section, :, hidden:] = gu_ref[section, :, hidden:]
        down = down_ref[section].astype(F32)
        level = jnp.sum(down, axis=-1, keepdims=True) * (1.0 / channels)
        down_v[section] = (down - level).astype(BF16)
    bias_w = bias_w_ref[...]
    square = (channels, channels)
    diagonal = lax.broadcasted_iota(jnp.int32, square, 0) == lax.broadcasted_iota(jnp.int32, square, 1)
    centring = (jnp.where(diagonal, 1.0, 0.0) - 1.0 / channels).astype(BF16)

    pair_step(0)
    send_bias(0, 0)
    for n in range(1, len(chunks)):
        if n == len(chunks) - 1:
            forward_kv(0, 0)
        pair_step(n)
        send_bias(n, 0)
    if len(chunks) == 1:
        forward_kv(0, 0)

    mask_row = mask_ref[...]
    real_count = jnp.sum(mask_row.astype(F32), axis=1, keepdims=True)
    is_real = mask_row == 1
    row_index = (lax.broadcasted_iota(jnp.int32, (rows, 1), 0) + pb * rows).astype(F32)
    row_real = (row_index < real_count).astype(F32)
    scale = 1.0 / HD**0.5

    def attend(layer, part):
        first, count = part
        keys_values = kv_all[layer].reshape(pb_count * rows, 2 * width)
        queries = query_gate[span(part)]
        lane = lax.broadcasted_iota(jnp.int32, (ROW_TILE, 2 * width), 1)
        tiles = range(0, count, ROW_TILE)
        spread_q = jnp.concatenate(
            [
                jnp.where(
                    (lane >= h * HD) & (lane < (h + 1) * HD), queries[t : t + ROW_TILE], jnp.zeros((), BF16)
                )
                for t in tiles
                for h in range(local_heads)
            ],
            axis=0,
        )
        scores = matmul_t(spread_q, keys_values) * scale
        wait_bias(layer, part)
        bias = jnp.concatenate(
            [
                bias_in[
                    source, layer, first // ROW_TILE : (first + count) // ROW_TILE
                ].reshape(local_heads * count, cols)
                for source in range(head_count)
            ],
            axis=1,
        )
        scores = scores + bias.astype(F32)
        scores = jnp.where(is_real, scores, -1e30)
        peak = jnp.max(scores, axis=1, keepdims=True)
        weights = jnp.exp(scores - peak)
        total = jnp.sum(weights, axis=1, keepdims=True)
        mixed = matmul(weights.astype(BF16), keys_values) / total
        rows_of = []
        for t in tiles:
            attended = jnp.zeros((ROW_TILE, 2 * width), F32)
            for h in range(local_heads):
                keep = (lane >= width + h * HD) & (lane < width + (h + 1) * HD)
                start = t * local_heads + h * ROW_TILE
                attended = attended + jnp.where(keep, mixed[start : start + ROW_TILE], 0.0)
            rows_of.append(attended)
        attended = jnp.concatenate(rows_of, axis=0)
        gated = (attended * jax.nn.sigmoid(queries.astype(F32))).astype(BF16)
        gated_all[layer, head, span(part)] = gated[:, width:]

    state_v[...] = tokens_ref[...].astype(F32)
    for layer in range(LAYERS):
        if layer:
            for p in range(len(kv_parts[layer])):
                forward_kv(layer, p)
        for p in range(len(kv_parts[layer])):
            finish_kv(layer, p)
        for p, part in enumerate(gated_parts[layer]):
            attend(layer, part)
            for k in range(1, head_count):
                gated_copy(layer, p, k).start()
            if not p:
                forward_out(layer)
        if layer + 1 < LAYERS:
            for n in range(len(chunks)):
                send_bias(n, layer + 1)
            for k in range(1, head_count):
                out_copy(layer + 1, k).start()
        wait_bytes(out_w.at[layer, 1:head_count, 0], out_fwd_recv.at[layer])
        for copy in own_out_copies(layer):
            copy.wait()
        last = layer == LAYERS - 1
        for p, part in enumerate([(0, rows)] if last else gated_parts[layer]):
            where = span(part)
            for q in range(len(gated_parts[layer])) if last else (p,):
                wait_bytes(
                    gated_all.at[layer, 1:head_count, span(gated_parts[layer][q])],
                    gated_recv.at[gated_index(layer, q)],
                )
            gathered = jnp.concatenate(
                [gated_all[layer, h, where] for h in range(head_count)], axis=1
            )
            update = matmul(gathered, out_w[layer].reshape(head_count * width, features))
            state = state_v[where] + row_real[where] * update
            if last:
                result_ref[where] = state.astype(BF16)
            else:
                if not p:
                    for copy in projection_copies(layer + 1):
                        copy.wait()
                state_v[where] = state
                normed = normalize(state).astype(BF16)
                project(layer + 1, p, normed)
                send_kv(layer + 1, p)
                project_own(layer + 1, p, normed)

    for layer in range(LAYERS):
        wait_bytes(bias_out.at[1:head_count, layer], bias_send.at[layer])
        wait_bytes(gated_all.at[layer, 1:head_count], gated_send.at[layer])
        wait_bytes(out_w.at[layer, 1:head_count, 0], out_send.at[layer])
        wait_bytes(out_w.at[layer, 1:head_count, 0], out_fwd_send.at[layer])
        wait_bytes(kv_all.at[layer, 1:chips], kv_send.at[layer])
        wait_bytes(kv_all.at[layer, :chips], fwd_send.at[layer])


def on_device(
    head_count, pb_count, pair, tokens, token_mask, w_gu, w_down, w_bias, w_q, w_k, w_v, w_gate, w_out
):
    rows, cols, channels = pair.shape
    width = w_q.shape[2]
    features = tokens.shape[1]
    local_heads = width // HD
    chips = pb_count // CORES
    chunks = len(pair_chunks(rows))
    kv_parts = 1 + (LAYERS - 1) * len(token_parts(rows))
    vmem = pl.BlockSpec(memory_space=pltpu.VMEM)
    anywhere = pl.BlockSpec(memory_space=pl.ANY)
    dma = pltpu.SemaphoreType.DMA
    bias_shape = (head_count, LAYERS, rows // ROW_TILE, local_heads, ROW_TILE, cols)
    return pl.pallas_call(
        functools.partial(step_kernel, head_count, pb_count),
        out_shape=pltpu.VMEM((rows, features), BF16),
        in_specs=[anywhere] * 11,
        out_specs=vmem,
        scratch_shapes=[
            pltpu.VMEM(tokens.shape, BF16),
            pltpu.VMEM((1, token_mask.shape[0]), jnp.int32),
            pltpu.VMEM(w_gu.shape, BF16),
            pltpu.VMEM(w_down.shape, BF16),
            pltpu.VMEM(w_bias.shape[::-1], BF16),
            pltpu.VMEM(pair.shape, BF16),
            pltpu.VMEM(w_gu.shape, BF16),
            pltpu.VMEM(w_down.shape, BF16),
            pltpu.VMEM((LAYERS, 4 * width, features), BF16),
            pltpu.VMEM((LAYERS, head_count, CORES, width // CORES, features), BF16),
            pltpu.VMEM(bias_shape, BF16),
            pltpu.VMEM(bias_shape, BF16),
            pltpu.VMEM((LAYERS, pb_count, rows, 2 * width), BF16),
            pltpu.VMEM((rows, 2 * width), BF16),
            pltpu.VMEM((LAYERS, head_count, rows, width), BF16),
            pltpu.VMEM((rows, features), F32),
            dma((5,)),
            dma((chunks,)),
            dma((LAYERS, 4 + CORES)),
            dma((LAYERS,)),
            dma((chunks, LAYERS)),
            dma((LAYERS,)),
            dma((kv_parts, chips - 1)),
            dma((LAYERS,)),
            dma((kv_parts,)),
            dma((LAYERS,)),
            dma((kv_parts,)),
            dma((LAYERS,)),
            dma((LAYERS,)),
            dma((LAYERS,)),
            dma((LAYERS,)),
        ],
        compiler_params=pltpu.CompilerParams(
            collective_id=0, has_side_effects=True, vmem_limit_bytes=60 * 1024 * 1024
        ),
        name="diffusion_step",
    )(
        pair,
        tokens,
        token_mask.reshape(1, -1),
        w_gu,
        w_down,
        w_bias.T,
        jnp.swapaxes(w_q, 1, 2),
        jnp.swapaxes(w_k, 1, 2),
        jnp.swapaxes(w_v, 1, 2),
        jnp.swapaxes(w_gate, 1, 2),
        w_out,
    )


def solution(mesh):
    placed = (
        P("pb", "head", None),
        P("pb", None),
        P(),
        P(),
        P(),
        P(),
        P(None, None, "head"),
        P(None, None, "head"),
        P(None, None, "head"),
        P(None, None, "head"),
        P(None, "head", None),
    )
    return jax.shard_map(
        functools.partial(on_device, mesh.shape["head"], mesh.shape["pb"]),
        mesh=mesh,
        in_specs=placed,
        out_specs=P("pb", None),
        check_vma=False,
    )
```

```python
import functools

import jax
import jax.numpy as jnp
from jax import lax
from jax.experimental import pallas as pl
from jax.experimental.pallas import tpu as pltpu
from jax.sharding import PartitionSpec as P

TRANS = 2
LAYERS = 2
HD = 48
CORES = 2
ROW_TILE = 16
GROUP = 8
LANES = 128
F32 = jnp.float32
BF16 = jnp.bfloat16


def normalize(values):
    inverse = 1.0 / values.shape[-1]
    center = values - jnp.sum(values, axis=-1, keepdims=True) * inverse
    spread = jnp.sum(center * center, axis=-1, keepdims=True) * inverse
    return center * lax.rsqrt(spread + 1e-05)


def scale_rows(center):
    inverse = 1.0 / center.shape[-1]
    spread = jnp.sum(center * center, axis=-1, keepdims=True) * inverse
    return (center * lax.rsqrt(spread + 1e-05)).astype(BF16)


def matmul(left, right):
    return jnp.dot(left, right, preferred_element_type=F32)


def matmul_t(left, right):
    return lax.dot_general(left, right, (((1,), (1,)), ((), ())), preferred_element_type=F32)


def pair_chunks(rows):
    tiles = rows // ROW_TILE
    counts = [1, tiles - 2, 1] if tiles > 2 else [1] * tiles
    starts = [sum(counts[:n]) for n in range(len(counts))]
    return [(a * ROW_TILE, c * ROW_TILE) for a, c in zip(starts, counts)]


def token_parts(rows):
    last = pair_chunks(rows)[-1][0]
    return [(0, last), (last, rows - last)]


def step_kernel(
    head_count,
    pb_count,
    pair_hbm,
    tokens_hbm,
    mask_hbm,
    gu_hbm,
    down_hbm,
    bias_w_hbm,
    q_hbm,
    k_hbm,
    v_hbm,
    gate_hbm,
    out_hbm,
    result_ref,
    tokens_ref,
    mask_ref,
    gu_ref,
    down_ref,
    bias_w_ref,
    pair_v,
    gu_v,
    down_v,
    wide_w,
    out_w,
    bias_out,
    bias_in,
    kv_all,
    query_gate,
    gated_all,
    state_v,
    small_sem,
    pair_sem,
    weight_sem,
    bias_send,
    bias_recv,
    kv_send,
    kv_recv,
    fwd_send,
    fwd_recv,
    gated_send,
    gated_recv,
    out_send,
    out_recv,
    out_fwd_send,
    out_fwd_recv,
):
    rows, cols, channels = pair_hbm.shape
    width = q_hbm.shape[1]
    features = tokens_hbm.shape[1]
    local_heads = width // HD
    heads_all = local_heads * head_count
    half_width = width // CORES
    chips = pb_count // CORES
    col_blocks = cols // LANES
    hidden = down_hbm.shape[1]
    chunks = pair_chunks(rows)
    parts = token_parts(rows)
    kv_parts = [[(0, rows)]] + [parts] * (LAYERS - 1)
    gated_parts = [parts] * (LAYERS - 1) + [[(0, rows)]]

    head = lax.axis_index("head")
    pb = lax.axis_index("pb")
    core = lax.rem(pb, CORES)
    chip = pb // CORES
    partner = chip * CORES + (1 - core)

    def head_peer(k):
        return lax.rem(head + k, head_count)

    def chip_peer(d):
        return lax.rem(chip + d, chips) * CORES + core

    def chip_source(d):
        return lax.rem(chip + chips - d, chips) * CORES + core

    def projection_copies(layer):
        return [
            pltpu.make_async_copy(
                source.at[layer],
                wide_w.at[layer, index * width : (index + 1) * width],
                weight_sem.at[layer, index],
            )
            for index, source in enumerate((k_hbm, v_hbm, q_hbm, gate_hbm))
        ]

    def own_out_copies(layer):
        return [
            pltpu.make_async_copy(
                out_hbm.at[layer, part * half_width : (part + 1) * half_width],
                out_w.at[layer, head, part],
                weight_sem.at[layer, 4 + part],
            )
            for part in range(CORES)
        ]

    def pair_copy(n):
        first, count = chunks[n]
        return pltpu.make_async_copy(
            pair_hbm.at[first : first + count], pair_v.at[first : first + count], pair_sem.at[n]
        )

    small = ((gu_hbm, gu_ref), (down_hbm, down_ref), (bias_w_hbm, bias_w_ref))
    small += ((tokens_hbm, tokens_ref), (mask_hbm, mask_ref))
    small_copies = [
        pltpu.make_async_copy(source, target, small_sem.at[n])
        for n, (source, target) in enumerate(small)
    ]
    first_weights = projection_copies(0)
    sooner = small_copies[3:4] + first_weights[:2]
    later = small_copies[4:] + first_weights[2:]
    for copy in sooner + [pair_copy(0)] + small_copies[:3] + later:
        copy.start()
    barrier = pltpu.get_barrier_semaphore()
    for k in range(1, head_count):
        pl.semaphore_signal(
            barrier, inc=1, device_id=(head_peer(k), pb), device_id_type=pl.DeviceIdType.MESH
        )
    for d in range(1, chips):
        pl.semaphore_signal(
            barrier, inc=1, device_id=(head, chip_peer(d)), device_id_type=pl.DeviceIdType.MESH
        )
    pl.semaphore_signal(
        barrier, inc=1, device_id=(head, partner), device_id_type=pl.DeviceIdType.MESH
    )

    for n in range(1, len(chunks)):
        pair_copy(n).start()
    for layer in range(LAYERS):
        for copy in own_out_copies(layer) + (projection_copies(layer) if layer else []):
            copy.start()

    def remote(source, target, send, recv, where):
        return pltpu.make_async_remote_copy(
            src_ref=source,
            dst_ref=target,
            send_sem=send,
            recv_sem=recv,
            device_id=where,
            device_id_type=pl.DeviceIdType.MESH,
        )

    def span(part):
        return slice(part[0], part[0] + part[1])

    def kv_index(layer, p):
        return sum(len(each) for each in kv_parts[:layer]) + p

    def gated_index(layer, p):
        return sum(len(each) for each in gated_parts[:layer]) + p

    def wait_bytes(block, semaphore):
        pltpu.make_async_copy(block, block, semaphore).wait()

    def kv_copy(layer, p, d):
        block = kv_all.at[layer, pb, span(kv_parts[layer][p])]
        return remote(
            block, block, kv_send.at[layer], kv_recv.at[kv_index(layer, p), d - 1], (head, chip_peer(d))
        )

    def kv_forward(layer, p, d):
        block = kv_all.at[layer, chip_source(d), span(kv_parts[layer][p])]
        return remote(
            block, block, fwd_send.at[layer], fwd_recv.at[kv_index(layer, p)], (head, partner)
        )

    def out_copy(layer, k):
        return remote(
            out_hbm.at[layer, pl.ds(pl.multiple_of(core * half_width, half_width), half_width)],
            out_w.at[layer, head, core],
            out_send.at[layer],
            out_recv.at[layer],
            (head_peer(k), pb),
        )

    def out_forward(layer, k):
        block = out_w.at[layer, lax.rem(head + head_count - k, head_count), core]
        return remote(
            block, block, out_fwd_send.at[layer], out_fwd_recv.at[layer], (head, partner)
        )

    def forward_out(layer):
        wait_bytes(out_w.at[layer, 1:head_count, 0], out_recv.at[layer])
        for k in range(1, head_count):
            out_forward(layer, k).start()

    def gated_copy(layer, p, k):
        block = gated_all.at[layer, head, span(gated_parts[layer][p])]
        return remote(
            block,
            block,
            gated_send.at[layer],
            gated_recv.at[gated_index(layer, p)],
            (head_peer(k), pb),
        )

    def bias_copy(n, layer, k):
        first, count = chunks[n]
        where = slice(first // ROW_TILE, (first + count) // ROW_TILE)
        return remote(
            bias_out.at[head_peer(k), layer, where],
            bias_in.at[head, layer, where],
            bias_send.at[layer],
            bias_recv.at[n, layer],
            (head_peer(k), pb),
        )

    def project(layer, p, normed):
        where = span(kv_parts[layer][p])
        kv_all[layer, pb, where] = matmul_t(normed, wide_w[layer, : 2 * width]).astype(BF16)

    def send_kv(layer, p):
        for d in range(1, chips):
            kv_copy(layer, p, d).start()
        kv_forward(layer, p, 0).start()

    def project_own(layer, p, normed):
        where = span(kv_parts[layer][p])
        query_gate[where] = matmul_t(normed, wide_w[layer, 2 * width :]).astype(BF16)

    def forward_kv(layer, p):
        for d in range(1, chips):
            kv_copy(layer, p, d).wait_recv()
            kv_forward(layer, p, d).start()

    def finish_kv(layer, p):
        wait_bytes(
            kv_all.at[layer, :chips, span(kv_parts[layer][p])], fwd_recv.at[kv_index(layer, p)]
        )

    def pair_block(first_row, row_count, first_col):
        blocks = []
        for start in range(0, row_count, GROUP):
            count = min(GROUP, row_count - start)
            block = pair_v[pl.ds(first_row + start, count), pl.ds(first_col, LANES), :]
            blocks.append(matmul(block.reshape(count * LANES, channels), centring))
        for section in range(TRANS):
            for n, center in enumerate(blocks):
                mixed = matmul(scale_rows(center), gu_v[section])
                gate = mixed[:, :hidden]
                units = ((gate + gate * jnp.tanh(gate)) * mixed[:, hidden:]).astype(BF16)
                blocks[n] = center + matmul(units, down_v[section])
        planes = []
        for center in blocks:
            projected = matmul_t(bias_w, scale_rows(center))
            planes += [
                projected[:, i : i + LANES] for i in range(0, projected.shape[1], LANES)
            ]
        by_head = jnp.transpose(jnp.stack(planes, axis=0), (1, 0, 2)).astype(BF16)
        for layer in range(LAYERS):
            for target in range(head_count):
                start = layer * heads_all + target * local_heads
                for row in range(0, row_count, ROW_TILE):
                    tile = (first_row + row) // ROW_TILE
                    bias_out[target, layer, tile, :, :, pl.ds(first_col, LANES)] = by_head[
                        start : start + local_heads, row : row + ROW_TILE
                    ]
        tiles = slice(first_row // ROW_TILE, (first_row + row_count) // ROW_TILE)
        bias_in[head, :, tiles, :, :, pl.ds(first_col, LANES)] = bias_out[
            head, :, tiles, :, :, pl.ds(first_col, LANES)
        ]

    def pair_step(n):
        pair_copy(n).wait()
        first_row, row_count = chunks[n]
        if col_blocks == 1:
            pair_block(first_row, row_count, 0)
        else:

            def one(block, carry):
                pair_block(first_row, row_count, pl.multiple_of(block * LANES, LANES))
                return carry

            lax.fori_loop(0, col_blocks, one, 0)

    def send_bias(n, layer):
        for k in range(1, head_count):
            bias_copy(n, layer, k).start()

    def wait_bias(layer, part):
        for n, (first, count) in enumerate(chunks):
            if part[0] <= first < part[0] + part[1]:
                tiles = slice(first // ROW_TILE, (first + count) // ROW_TILE)
                wait_bytes(bias_in.at[1:head_count, layer, tiles], bias_recv.at[n, layer])

    for copy in sooner:
        copy.wait()
    normed = normalize(tokens_ref[...].astype(F32)).astype(BF16)
    project(0, 0, normed)
    pl.semaphore_wait(barrier, head_count + chips - 1)
    send_kv(0, 0)
    for k in range(1, head_count):
        out_copy(0, k).start()
    for copy in small_copies[:3]:
        copy.wait()
    for section in range(TRANS):
        gu_v[section, :, :hidden] = (gu_ref[section, :, :hidden].astype(F32) * 0.5).astype(BF16)
        gu_v[section, :, hidden:] = gu_ref[section, :, hidden:]
        down = down_ref[section].astype(F32)
        level = jnp.sum(down, axis=-1, keepdims=True) * (1.0 / channels)
        down_v[section] = (down - level).astype(BF16)
    bias_w = bias_w_ref[...]
    square = (channels, channels)
    diagonal = lax.broadcasted_iota(jnp.int32, square, 0) == lax.broadcasted_iota(jnp.int32, square, 1)
    centring = (jnp.where(diagonal, 1.0, 0.0) - 1.0 / channels).astype(BF16)

    pair_step(0)
    send_bias(0, 0)
    for n in range(1, len(chunks)):
        if n == len(chunks) - 1:
            forward_kv(0, 0)
        pair_step(n)
        send_bias(n, 0)
    if len(chunks) == 1:
        forward_kv(0, 0)
    for copy in later:
        copy.wait()
    project_own(0, 0, normed)

    mask_row = mask_ref[...]
    real_count = jnp.sum(mask_row.astype(F32), axis=1, keepdims=True)
    is_real = mask_row == 1
    row_index = (lax.broadcasted_iota(jnp.int32, (rows, 1), 0) + pb * rows).astype(F32)
    row_real = (row_index < real_count).astype(F32)
    scale = 1.0 / HD**0.5

    def attend(layer, part):
        first, count = part
        keys_values = kv_all[layer].reshape(pb_count * rows, 2 * width)
        queries = query_gate[span(part)]
        lane = lax.broadcasted_iota(jnp.int32, (ROW_TILE, 2 * width), 1)
        tiles = range(0, count, ROW_TILE)
        spread_q = jnp.concatenate(
            [
                jnp.where(
                    (lane >= h * HD) & (lane < (h + 1) * HD), queries[t : t + ROW_TILE], jnp.zeros((), BF16)
                )
                for t in tiles
                for h in range(local_heads)
            ],
            axis=0,
        )
        scores = matmul_t(spread_q, keys_values) * scale
        wait_bias(layer, part)
        bias = jnp.concatenate(
            [
                bias_in[
                    source, layer, first // ROW_TILE : (first + count) // ROW_TILE
                ].reshape(local_heads * count, cols)
                for source in range(head_count)
            ],
            axis=1,
        )
        scores = scores + bias.astype(F32)
        scores = jnp.where(is_real, scores, -1e30)
        peak = jnp.max(scores, axis=1, keepdims=True)
        weights = jnp.exp(scores - peak)
        total = jnp.sum(weights, axis=1, keepdims=True)
        mixed = matmul(weights.astype(BF16), keys_values) / total
        rows_of = []
        for t in tiles:
            attended = jnp.zeros((ROW_TILE, 2 * width), F32)
            for h in range(local_heads):
                keep = (lane >= width + h * HD) & (lane < width + (h + 1) * HD)
                start = t * local_heads + h * ROW_TILE
                attended = attended + jnp.where(keep, mixed[start : start + ROW_TILE], 0.0)
            rows_of.append(attended)
        attended = jnp.concatenate(rows_of, axis=0)
        gated = (attended * jax.nn.sigmoid(queries.astype(F32))).astype(BF16)
        gated_all[layer, head, span(part)] = gated[:, width:]

    state_v[...] = tokens_ref[...].astype(F32)
    for layer in range(LAYERS):
        if layer:
            for p in range(len(kv_parts[layer])):
                forward_kv(layer, p)
        for p in range(len(kv_parts[layer])):
            finish_kv(layer, p)
        for p, part in enumerate(gated_parts[layer]):
            attend(layer, part)
            for k in range(1, head_count):
                gated_copy(layer, p, k).start()
            if not p:
                forward_out(layer)
        if layer + 1 < LAYERS:
            for n in range(len(chunks)):
                send_bias(n, layer + 1)
            for k in range(1, head_count):
                out_copy(layer + 1, k).start()
        wait_bytes(out_w.at[layer, 1:head_count, 0], out_fwd_recv.at[layer])
        for copy in own_out_copies(layer):
            copy.wait()
        last = layer == LAYERS - 1
        for p, part in enumerate([(0, rows)] if last else gated_parts[layer]):
            where = span(part)
            for q in range(len(gated_parts[layer])) if last else (p,):
                wait_bytes(
                    gated_all.at[layer, 1:head_count, span(gated_parts[layer][q])],
                    gated_recv.at[gated_index(layer, q)],
                )
            gathered = jnp.concatenate(
                [gated_all[layer, h, where] for h in range(head_count)], axis=1
            )
            update = matmul(gathered, out_w[layer].reshape(head_count * width, features))
            state = state_v[where] + row_real[where] * update
            if last:
                result_ref[where] = state.astype(BF16)
            else:
                if not p:
                    for copy in projection_copies(layer + 1):
                        copy.wait()
                state_v[where] = state
                normed = normalize(state).astype(BF16)
                project(layer + 1, p, normed)
                send_kv(layer + 1, p)
                project_own(layer + 1, p, normed)

    for layer in range(LAYERS):
        wait_bytes(bias_out.at[1:head_count, layer], bias_send.at[layer])
        wait_bytes(gated_all.at[layer, 1:head_count], gated_send.at[layer])
        wait_bytes(out_w.at[layer, 1:head_count, 0], out_send.at[layer])
        wait_bytes(out_w.at[layer, 1:head_count, 0], out_fwd_send.at[layer])
        wait_bytes(kv_all.at[layer, 1:chips], kv_send.at[layer])
        wait_bytes(kv_all.at[layer, :chips], fwd_send.at[layer])


def on_device(
    head_count, pb_count, pair, tokens, token_mask, w_gu, w_down, w_bias, w_q, w_k, w_v, w_gate, w_out
):
    rows, cols, channels = pair.shape
    width = w_q.shape[2]
    features = tokens.shape[1]
    local_heads = width // HD
    chips = pb_count // CORES
    chunks = len(pair_chunks(rows))
    kv_parts = 1 + (LAYERS - 1) * len(token_parts(rows))
    vmem = pl.BlockSpec(memory_space=pltpu.VMEM)
    anywhere = pl.BlockSpec(memory_space=pl.ANY)
    dma = pltpu.SemaphoreType.DMA
    bias_shape = (head_count, LAYERS, rows // ROW_TILE, local_heads, ROW_TILE, cols)
    return pl.pallas_call(
        functools.partial(step_kernel, head_count, pb_count),
        out_shape=pltpu.VMEM((rows, features), BF16),
        in_specs=[anywhere] * 11,
        out_specs=vmem,
        scratch_shapes=[
            pltpu.VMEM(tokens.shape, BF16),
            pltpu.VMEM((1, token_mask.shape[0]), jnp.int32),
            pltpu.VMEM(w_gu.shape, BF16),
            pltpu.VMEM(w_down.shape, BF16),
            pltpu.VMEM(w_bias.shape[::-1], BF16),
            pltpu.VMEM(pair.shape, BF16),
            pltpu.VMEM(w_gu.shape, BF16),
            pltpu.VMEM(w_down.shape, BF16),
            pltpu.VMEM((LAYERS, 4 * width, features), BF16),
            pltpu.VMEM((LAYERS, head_count, CORES, width // CORES, features), BF16),
            pltpu.VMEM(bias_shape, BF16),
            pltpu.VMEM(bias_shape, BF16),
            pltpu.VMEM((LAYERS, pb_count, rows, 2 * width), BF16),
            pltpu.VMEM((rows, 2 * width), BF16),
            pltpu.VMEM((LAYERS, head_count, rows, width), BF16),
            pltpu.VMEM((rows, features), F32),
            dma((5,)),
            dma((chunks,)),
            dma((LAYERS, 4 + CORES)),
            dma((LAYERS,)),
            dma((chunks, LAYERS)),
            dma((LAYERS,)),
            dma((kv_parts, chips - 1)),
            dma((LAYERS,)),
            dma((kv_parts,)),
            dma((LAYERS,)),
            dma((kv_parts,)),
            dma((LAYERS,)),
            dma((LAYERS,)),
            dma((LAYERS,)),
            dma((LAYERS,)),
        ],
        compiler_params=pltpu.CompilerParams(
            collective_id=0, has_side_effects=True, vmem_limit_bytes=60 * 1024 * 1024
        ),
        name="diffusion_step",
    )(
        pair,
        tokens,
        token_mask.reshape(1, -1),
        w_gu,
        w_down,
        w_bias.T,
        jnp.swapaxes(w_q, 1, 2),
        jnp.swapaxes(w_k, 1, 2),
        jnp.swapaxes(w_v, 1, 2),
        jnp.swapaxes(w_gate, 1, 2),
        w_out,
    )


def solution(mesh):
    placed = (
        P("pb", "head", None),
        P("pb", None),
        P(),
        P(),
        P(),
        P(),
        P(None, None, "head"),
        P(None, None, "head"),
        P(None, None, "head"),
        P(None, None, "head"),
        P(None, "head", None),
    )
    return jax.shard_map(
        functools.partial(on_device, mesh.shape["head"], mesh.shape["pb"]),
        mesh=mesh,
        in_specs=placed,
        out_specs=P("pb", None),
        check_vma=False,
    )
```

```python
import functools

import jax
import jax.numpy as jnp
from jax import lax
from jax.experimental import pallas as pl
from jax.experimental.pallas import tpu as pltpu
from jax.sharding import PartitionSpec as P

TRANS = 2
LAYERS = 2
HD = 48
CORES = 2
ROW_TILE = 16
GROUP = 16
LANES = 128
F32 = jnp.float32
BF16 = jnp.bfloat16


def normalize(values):
    inverse = 1.0 / values.shape[-1]
    center = values - jnp.sum(values, axis=-1, keepdims=True) * inverse
    spread = jnp.sum(center * center, axis=-1, keepdims=True) * inverse
    return center * lax.rsqrt(spread + 1e-05)


def scale_rows(center):
    inverse = 1.0 / center.shape[-1]
    spread = jnp.sum(center * center, axis=-1, keepdims=True) * inverse
    return (center * lax.rsqrt(spread + 1e-05)).astype(BF16)


def matmul(left, right):
    return jnp.dot(left, right, preferred_element_type=F32)


def matmul_t(left, right):
    return lax.dot_general(left, right, (((1,), (1,)), ((), ())), preferred_element_type=F32)


def pair_chunks(rows):
    tiles = rows // ROW_TILE
    counts = [tiles - 1, 1] if tiles > 1 else [1]
    starts = [sum(counts[:n]) for n in range(len(counts))]
    return [(a * ROW_TILE, c * ROW_TILE) for a, c in zip(starts, counts)]


def token_parts(rows):
    last = pair_chunks(rows)[-1][0]
    return [(0, last), (last, rows - last)]


def step_kernel(
    head_count,
    pb_count,
    pair_hbm,
    tokens_hbm,
    mask_hbm,
    gu_hbm,
    down_hbm,
    bias_w_hbm,
    q_hbm,
    k_hbm,
    v_hbm,
    gate_hbm,
    out_hbm,
    result_ref,
    tokens_ref,
    mask_ref,
    gu_ref,
    down_ref,
    bias_w_ref,
    pair_v,
    gu_v,
    down_v,
    wide_w,
    out_w,
    bias_out,
    bias_in,
    kv_all,
    query_gate,
    gated_all,
    state_v,
    small_sem,
    pair_sem,
    weight_sem,
    bias_send,
    bias_recv,
    kv_send,
    kv_recv,
    fwd_send,
    fwd_recv,
    gated_send,
    gated_recv,
    out_send,
    out_recv,
    out_fwd_send,
    out_fwd_recv,
):
    rows, cols, channels = pair_hbm.shape
    width = q_hbm.shape[1]
    features = tokens_hbm.shape[1]
    local_heads = width // HD
    heads_all = local_heads * head_count
    half_width = width // CORES
    chips = pb_count // CORES
    col_blocks = cols // LANES
    hidden = down_hbm.shape[1]
    chunks = pair_chunks(rows)
    parts = token_parts(rows)
    kv_parts = [[(0, rows)]] + [parts] * (LAYERS - 1)
    gated_parts = [parts] * (LAYERS - 1) + [[(0, rows)]]

    head = lax.axis_index("head")
    pb = lax.axis_index("pb")
    core = lax.rem(pb, CORES)
    chip = pb // CORES
    partner = chip * CORES + (1 - core)

    def head_peer(k):
        return lax.rem(head + k, head_count)

    def chip_peer(d):
        return lax.rem(chip + d, chips) * CORES + core

    def chip_source(d):
        return lax.rem(chip + chips - d, chips) * CORES + core

    def projection_copies(layer):
        return [
            pltpu.make_async_copy(
                source.at[layer],
                wide_w.at[layer, index * width : (index + 1) * width],
                weight_sem.at[layer, index],
            )
            for index, source in enumerate((k_hbm, v_hbm, q_hbm, gate_hbm))
        ]

    def own_out_copies(layer):
        return [
            pltpu.make_async_copy(
                out_hbm.at[layer, part * half_width : (part + 1) * half_width],
                out_w.at[layer, head, part],
                weight_sem.at[layer, 4 + part],
            )
            for part in range(CORES)
        ]

    def pair_copy(n):
        first, count = chunks[n]
        return pltpu.make_async_copy(
            pair_hbm.at[first : first + count], pair_v.at[first : first + count], pair_sem.at[n]
        )

    small = ((gu_hbm, gu_ref), (down_hbm, down_ref), (bias_w_hbm, bias_w_ref))
    small += ((tokens_hbm, tokens_ref), (mask_hbm, mask_ref))
    small_copies = [
        pltpu.make_async_copy(source, target, small_sem.at[n])
        for n, (source, target) in enumerate(small)
    ]
    first_weights = projection_copies(0)
    sooner = small_copies[3:4] + first_weights[:2]
    later = small_copies[4:] + first_weights[2:]
    for copy in sooner + [pair_copy(0)] + small_copies[:3] + later:
        copy.start()
    barrier = pltpu.get_barrier_semaphore()
    for k in range(1, head_count):
        pl.semaphore_signal(
            barrier, inc=1, device_id=(head_peer(k), pb), device_id_type=pl.DeviceIdType.MESH
        )
    for d in range(1, chips):
        pl.semaphore_signal(
            barrier, inc=1, device_id=(head, chip_peer(d)), device_id_type=pl.DeviceIdType.MESH
        )
    pl.semaphore_signal(
        barrier, inc=1, device_id=(head, partner), device_id_type=pl.DeviceIdType.MESH
    )

    for n in range(1, len(chunks)):
        pair_copy(n).start()
    for layer in range(LAYERS):
        for copy in own_out_copies(layer) + (projection_copies(layer) if layer else []):
            copy.start()

    def remote(source, target, send, recv, where):
        return pltpu.make_async_remote_copy(
            src_ref=source,
            dst_ref=target,
            send_sem=send,
            recv_sem=recv,
            device_id=where,
            device_id_type=pl.DeviceIdType.MESH,
        )

    def span(part):
        return slice(part[0], part[0] + part[1])

    def kv_index(layer, p):
        return sum(len(each) for each in kv_parts[:layer]) + p

    def gated_index(layer, p):
        return sum(len(each) for each in gated_parts[:layer]) + p

    def wait_bytes(block, semaphore):
        pltpu.make_async_copy(block, block, semaphore).wait()

    def kv_copy(layer, p, d):
        block = kv_all.at[layer, pb, span(kv_parts[layer][p])]
        return remote(
            block, block, kv_send.at[layer], kv_recv.at[kv_index(layer, p), d - 1], (head, chip_peer(d))
        )

    def kv_forward(layer, p, d):
        block = kv_all.at[layer, chip_source(d), span(kv_parts[layer][p])]
        return remote(
            block, block, fwd_send.at[layer], fwd_recv.at[kv_index(layer, p)], (head, partner)
        )

    def out_copy(layer, k):
        return remote(
            out_hbm.at[layer, pl.ds(pl.multiple_of(core * half_width, half_width), half_width)],
            out_w.at[layer, head, core],
            out_send.at[layer],
            out_recv.at[layer],
            (head_peer(k), pb),
        )

    def out_forward(layer, k):
        block = out_w.at[layer, lax.rem(head + head_count - k, head_count), core]
        return remote(
            block, block, out_fwd_send.at[layer], out_fwd_recv.at[layer], (head, partner)
        )

    def forward_out(layer):
        wait_bytes(out_w.at[layer, 1:head_count, 0], out_recv.at[layer])
        for k in range(1, head_count):
            out_forward(layer, k).start()

    def gated_copy(layer, p, k):
        block = gated_all.at[layer, head, span(gated_parts[layer][p])]
        return remote(
            block,
            block,
            gated_send.at[layer],
            gated_recv.at[gated_index(layer, p)],
            (head_peer(k), pb),
        )

    def bias_copy(n, layer, k):
        first, count = chunks[n]
        where = slice(first // ROW_TILE, (first + count) // ROW_TILE)
        return remote(
            bias_out.at[head_peer(k), layer, where],
            bias_in.at[head, layer, where],
            bias_send.at[layer],
            bias_recv.at[n, layer],
            (head_peer(k), pb),
        )

    def project(layer, p, normed):
        where = span(kv_parts[layer][p])
        kv_all[layer, pb, where] = matmul_t(normed, wide_w[layer, : 2 * width]).astype(BF16)

    def send_kv(layer, p):
        for d in range(1, chips):
            kv_copy(layer, p, d).start()
        kv_forward(layer, p, 0).start()

    def project_own(layer, p, normed):
        where = span(kv_parts[layer][p])
        query_gate[where] = matmul_t(normed, wide_w[layer, 2 * width :]).astype(BF16)

    def forward_kv(layer, p):
        for d in range(1, chips):
            kv_copy(layer, p, d).wait_recv()
            kv_forward(layer, p, d).start()

    def finish_kv(layer, p):
        wait_bytes(
            kv_all.at[layer, :chips, span(kv_parts[layer][p])], fwd_recv.at[kv_index(layer, p)]
        )

    def pair_block(first_row, row_count, first_col):
        blocks = []
        for start in range(0, row_count, GROUP):
            count = min(GROUP, row_count - start)
            block = pair_v[pl.ds(first_row + start, count), pl.ds(first_col, LANES), :]
            blocks.append(matmul(block.reshape(count * LANES, channels), centring))
        for section in range(TRANS):
            for n, center in enumerate(blocks):
                mixed = matmul(scale_rows(center), gu_v[section])
                gate = mixed[:, :hidden]
                units = ((gate + gate * jnp.tanh(gate)) * mixed[:, hidden:]).astype(BF16)
                blocks[n] = center + matmul(units, down_v[section])
        planes = []
        for center in blocks:
            projected = matmul_t(bias_w, scale_rows(center))
            planes += [
                projected[:, i : i + LANES] for i in range(0, projected.shape[1], LANES)
            ]
        by_head = jnp.transpose(jnp.stack(planes, axis=0), (1, 0, 2)).astype(BF16)
        for layer in range(LAYERS):
            for target in range(head_count):
                start = layer * heads_all + target * local_heads
                for row in range(0, row_count, ROW_TILE):
                    tile = (first_row + row) // ROW_TILE
                    bias_out[target, layer, tile, :, :, pl.ds(first_col, LANES)] = by_head[
                        start : start + local_heads, row : row + ROW_TILE
                    ]
        tiles = slice(first_row // ROW_TILE, (first_row + row_count) // ROW_TILE)
        bias_in[head, :, tiles, :, :, pl.ds(first_col, LANES)] = bias_out[
            head, :, tiles, :, :, pl.ds(first_col, LANES)
        ]

    def pair_step(n):
        pair_copy(n).wait()
        first_row, row_count = chunks[n]
        if col_blocks == 1:
            pair_block(first_row, row_count, 0)
        else:

            def one(block, carry):
                pair_block(first_row, row_count, pl.multiple_of(block * LANES, LANES))
                return carry

            lax.fori_loop(0, col_blocks, one, 0)

    def send_bias(n, layer):
        for k in range(1, head_count):
            bias_copy(n, layer, k).start()

    def wait_bias(layer, part):
        for n, (first, count) in enumerate(chunks):
            if part[0] <= first < part[0] + part[1]:
                tiles = slice(first // ROW_TILE, (first + count) // ROW_TILE)
                wait_bytes(bias_in.at[1:head_count, layer, tiles], bias_recv.at[n, layer])

    for copy in sooner:
        copy.wait()
    normed = normalize(tokens_ref[...].astype(F32)).astype(BF16)
    project(0, 0, normed)
    pl.semaphore_wait(barrier, head_count + chips - 1)
    send_kv(0, 0)
    for k in range(1, head_count):
        out_copy(0, k).start()
    for copy in small_copies[:3]:
        copy.wait()
    for section in range(TRANS):
        gu_v[section, :, :hidden] = (gu_ref[section, :, :hidden].astype(F32) * 0.5).astype(BF16)
        gu_v[section, :, hidden:] = gu_ref[section, :, hidden:]
        down = down_ref[section].astype(F32)
        level = jnp.sum(down, axis=-1, keepdims=True) * (1.0 / channels)
        down_v[section] = (down - level).astype(BF16)
    bias_w = bias_w_ref[...]
    square = (channels, channels)
    diagonal = lax.broadcasted_iota(jnp.int32, square, 0) == lax.broadcasted_iota(jnp.int32, square, 1)
    centring = (jnp.where(diagonal, 1.0, 0.0) - 1.0 / channels).astype(BF16)

    pair_step(0)
    send_bias(0, 0)
    for n in range(1, len(chunks)):
        if n == len(chunks) - 1:
            forward_kv(0, 0)
        pair_step(n)
        send_bias(n, 0)
    if len(chunks) == 1:
        forward_kv(0, 0)
    for copy in later:
        copy.wait()
    project_own(0, 0, normed)

    mask_row = mask_ref[...]
    real_count = jnp.sum(mask_row.astype(F32), axis=1, keepdims=True)
    is_real = mask_row == 1
    row_index = (lax.broadcasted_iota(jnp.int32, (rows, 1), 0) + pb * rows).astype(F32)
    row_real = (row_index < real_count).astype(F32)
    scale = 1.0 / HD**0.5

    def attend(layer, part):
        first, count = part
        keys_values = kv_all[layer].reshape(pb_count * rows, 2 * width)
        queries = query_gate[span(part)]
        lane = lax.broadcasted_iota(jnp.int32, (ROW_TILE, 2 * width), 1)
        tiles = range(0, count, ROW_TILE)
        spread_q = jnp.concatenate(
            [
                jnp.where(
                    (lane >= h * HD) & (lane < (h + 1) * HD), queries[t : t + ROW_TILE], jnp.zeros((), BF16)
                )
                for t in tiles
                for h in range(local_heads)
            ],
            axis=0,
        )
        scores = matmul_t(spread_q, keys_values) * scale
        wait_bias(layer, part)
        bias = jnp.concatenate(
            [
                bias_in[
                    source, layer, first // ROW_TILE : (first + count) // ROW_TILE
                ].reshape(local_heads * count, cols)
                for source in range(head_count)
            ],
            axis=1,
        )
        scores = scores + bias.astype(F32)
        scores = jnp.where(is_real, scores, -1e30)
        peak = jnp.max(scores, axis=1, keepdims=True)
        weights = jnp.exp(scores - peak)
        total = jnp.sum(weights, axis=1, keepdims=True)
        mixed = matmul(weights.astype(BF16), keys_values) / total
        rows_of = []
        for t in tiles:
            attended = jnp.zeros((ROW_TILE, 2 * width), F32)
            for h in range(local_heads):
                keep = (lane >= width + h * HD) & (lane < width + (h + 1) * HD)
                start = t * local_heads + h * ROW_TILE
                attended = attended + jnp.where(keep, mixed[start : start + ROW_TILE], 0.0)
            rows_of.append(attended)
        attended = jnp.concatenate(rows_of, axis=0)
        gated = (attended * jax.nn.sigmoid(queries.astype(F32))).astype(BF16)
        gated_all[layer, head, span(part)] = gated[:, width:]

    state_v[...] = tokens_ref[...].astype(F32)
    for layer in range(LAYERS):
        if layer:
            for p in range(len(kv_parts[layer])):
                forward_kv(layer, p)
        for p in range(len(kv_parts[layer])):
            finish_kv(layer, p)
        for p, part in enumerate(gated_parts[layer]):
            attend(layer, part)
            for k in range(1, head_count):
                gated_copy(layer, p, k).start()
            if not p:
                forward_out(layer)
        if layer + 1 < LAYERS:
            for n in range(len(chunks)):
                send_bias(n, layer + 1)
            for k in range(1, head_count):
                out_copy(layer + 1, k).start()
        wait_bytes(out_w.at[layer, 1:head_count, 0], out_fwd_recv.at[layer])
        for copy in own_out_copies(layer):
            copy.wait()
        last = layer == LAYERS - 1
        for p, part in enumerate([(0, rows)] if last else gated_parts[layer]):
            where = span(part)
            for q in range(len(gated_parts[layer])) if last else (p,):
                wait_bytes(
                    gated_all.at[layer, 1:head_count, span(gated_parts[layer][q])],
                    gated_recv.at[gated_index(layer, q)],
                )
            gathered = jnp.concatenate(
                [gated_all[layer, h, where] for h in range(head_count)], axis=1
            )
            update = matmul(gathered, out_w[layer].reshape(head_count * width, features))
            state = state_v[where] + row_real[where] * update
            if last:
                result_ref[where] = state.astype(BF16)
            else:
                if not p:
                    for copy in projection_copies(layer + 1):
                        copy.wait()
                state_v[where] = state
                normed = normalize(state).astype(BF16)
                project(layer + 1, p, normed)
                send_kv(layer + 1, p)
                project_own(layer + 1, p, normed)

    for layer in range(LAYERS):
        wait_bytes(bias_out.at[1:head_count, layer], bias_send.at[layer])
        wait_bytes(gated_all.at[layer, 1:head_count], gated_send.at[layer])
        wait_bytes(out_w.at[layer, 1:head_count, 0], out_send.at[layer])
        wait_bytes(out_w.at[layer, 1:head_count, 0], out_fwd_send.at[layer])
        wait_bytes(kv_all.at[layer, 1:chips], kv_send.at[layer])
        wait_bytes(kv_all.at[layer, :chips], fwd_send.at[layer])


def on_device(
    head_count, pb_count, pair, tokens, token_mask, w_gu, w_down, w_bias, w_q, w_k, w_v, w_gate, w_out
):
    rows, cols, channels = pair.shape
    width = w_q.shape[2]
    features = tokens.shape[1]
    local_heads = width // HD
    chips = pb_count // CORES
    chunks = len(pair_chunks(rows))
    kv_parts = 1 + (LAYERS - 1) * len(token_parts(rows))
    vmem = pl.BlockSpec(memory_space=pltpu.VMEM)
    anywhere = pl.BlockSpec(memory_space=pl.ANY)
    dma = pltpu.SemaphoreType.DMA
    bias_shape = (head_count, LAYERS, rows // ROW_TILE, local_heads, ROW_TILE, cols)
    return pl.pallas_call(
        functools.partial(step_kernel, head_count, pb_count),
        out_shape=pltpu.VMEM((rows, features), BF16),
        in_specs=[anywhere] * 11,
        out_specs=vmem,
        scratch_shapes=[
            pltpu.VMEM(tokens.shape, BF16),
            pltpu.VMEM((1, token_mask.shape[0]), jnp.int32),
            pltpu.VMEM(w_gu.shape, BF16),
            pltpu.VMEM(w_down.shape, BF16),
            pltpu.VMEM(w_bias.shape[::-1], BF16),
            pltpu.VMEM(pair.shape, BF16),
            pltpu.VMEM(w_gu.shape, BF16),
            pltpu.VMEM(w_down.shape, BF16),
            pltpu.VMEM((LAYERS, 4 * width, features), BF16),
            pltpu.VMEM((LAYERS, head_count, CORES, width // CORES, features), BF16),
            pltpu.VMEM(bias_shape, BF16),
            pltpu.VMEM(bias_shape, BF16),
            pltpu.VMEM((LAYERS, pb_count, rows, 2 * width), BF16),
            pltpu.VMEM((rows, 2 * width), BF16),
            pltpu.VMEM((LAYERS, head_count, rows, width), BF16),
            pltpu.VMEM((rows, features), F32),
            dma((5,)),
            dma((chunks,)),
            dma((LAYERS, 4 + CORES)),
            dma((LAYERS,)),
            dma((chunks, LAYERS)),
            dma((LAYERS,)),
            dma((kv_parts, chips - 1)),
            dma((LAYERS,)),
            dma((kv_parts,)),
            dma((LAYERS,)),
            dma((kv_parts,)),
            dma((LAYERS,)),
            dma((LAYERS,)),
            dma((LAYERS,)),
            dma((LAYERS,)),
        ],
        compiler_params=pltpu.CompilerParams(
            collective_id=0, has_side_effects=True, vmem_limit_bytes=60 * 1024 * 1024
        ),
        name="diffusion_step",
    )(
        pair,
        tokens,
        token_mask.reshape(1, -1),
        w_gu,
        w_down,
        w_bias.T,
        jnp.swapaxes(w_q, 1, 2),
        jnp.swapaxes(w_k, 1, 2),
        jnp.swapaxes(w_v, 1, 2),
        jnp.swapaxes(w_gate, 1, 2),
        w_out,
    )


def solution(mesh):
    placed = (
        P("pb", "head", None),
        P("pb", None),
        P(),
        P(),
        P(),
        P(),
        P(None, None, "head"),
        P(None, None, "head"),
        P(None, None, "head"),
        P(None, None, "head"),
        P(None, "head", None),
    )
    return jax.shard_map(
        functools.partial(on_device, mesh.shape["head"], mesh.shape["pb"]),
        mesh=mesh,
        in_specs=placed,
        out_specs=P("pb", None),
        check_vma=False,
    )
```
